32 devices in a mesh: section: 2 (over core), ha: 4 (over z), wa: 4 (over y, x).
Axes of the slice: x: 2, y: 2, z: 4, core: 2. Of those that a mesh axis runs over, the one named last changes fastest.
Arguments:
- queries: bfloat16 [2, 1, 32, 64, 1536], P('section', None, 'ha', 'wa'), may hold values from -85 to 85
- keys: bfloat16 [2, 1, 32, 64, 1536], P('section', None, 'ha', 'wa'), may hold values from -4.5 to 4.5
- values: bfloat16 [2, 1, 32, 64, 1536], P('section', None, 'ha', 'wa'), may hold values from -6 to 6
- cotangent: bfloat16 [2, 1, 32, 64, 1536], P('section', None, 'ha', 'wa'), may hold values from -6 to 6
- upstream: bfloat16 [2, 1, 32, 64, 1536], P('section', None, 'ha', 'wa'), may hold values from -6 to 6
- block_mask: int32 [2, 4, 8, 9], P('section', 'ha', 'wa'), may hold values from 0 to 1, as said below
Outputs:
- grad_queries: bfloat16 [2, 1, 32, 64, 1536], P('section', None, 'ha', 'wa')
- grad_keys: bfloat16 [2, 1, 32, 64, 1536], P('section', None, 'ha', 'wa')
- grad_values: bfloat16 [2, 1, 32, 64, 1536], P('section', None, 'ha', 'wa')
The draws below stay inside these ranges and needn't reach their ends.
Inputs may be any that keep to these rules, and one draw needn't show every extreme that they name: `block_mask`: entry 4, the tile's own block, is always 1.
All inputs are finite; a program needn't handle non-finite values.
Results may differ from the reference program's by a relative error of at most 0.0068.
Values may be sent and summed in bfloat16 or wider, within the bound.
A program may use at most 64 MiB of HBM per device.

```python
import jax
import jax.numpy as jnp
from jax import lax

HEADS = 12
HEAD_DIM = 128
TILE = 8
SPAN_TILES = 2
FRAMES = 1
SECTIONS = 2
TILE_ROWS = 4
TILE_COLS = 8
HEIGHT = 32
WIDTH = 64
CHANNELS = 1536


def pair_fields(key):
    base_key = jax.random.fold_in(key, 5)
    key_a, key_b = jax.random.split(base_key, 2)
    field_shape = (SECTIONS, FRAMES, HEIGHT, WIDTH, CHANNELS)
    key_field = jnp.clip(jax.random.normal(key_b, field_shape, jnp.float32), -4.0, 4.0)
    query_field = jnp.clip(jax.random.normal(key_a, field_shape, jnp.float32), -4.0, 4.0)
    return (query_field, key_field)


def draw_queries(key, part):
    query_field, key_field = pair_fields(key)
    return query_field.astype(jnp.bfloat16)


def draw_keys(key, part):
    query_field, key_field = pair_fields(key)
    return key_field.astype(jnp.bfloat16)


def draw_block_mask(key, part):
    mask_key = jax.random.fold_in(key, 11)
    picks = jax.random.randint(mask_key, (SECTIONS, TILE_ROWS, TILE_COLS, 9), 0, 4)
    center = jnp.arange(9, dtype=jnp.int32) == 4
    return jnp.where(center[None, None, None, :], 1, (picks > 0).astype(jnp.int32)).astype(jnp.int32)


def block_levels(own_key, dims, cuts, smallest, high):
    def one(dim, shards_of):
        heights = jax.random.uniform(jax.random.fold_in(jax.random.fold_in(own_key, 6), dim), (shards_of,), jnp.float32, smallest / len(cuts), high / len(cuts))
        return jnp.repeat(jnp.exp(heights), dims[dim] // shards_of).reshape((-1,) + (1,) * (len(dims) - dim - 1))

    factor_of = one(*cuts[0])
    for cut in cuts[1:]:
        factor_of = factor_of * one(*cut)
    return factor_of


def noise(own_key, extent, width, limit, cuts=(), held_as=jnp.bfloat16):
    level = block_levels(own_key, extent, cuts, -0.22, 0.18) if cuts else 1.0
    result = jax.random.normal(own_key, extent, jnp.float32) * width * level
    return jnp.minimum(jnp.maximum(result, -limit), limit).astype(held_as)


def setup_inputs(seed: int = 0) -> dict:
    splits = jax.random.split(jax.random.key(seed), 7)
    return {
        "queries": draw_queries(jax.random.fold_in(splits[6], 71), 0),
        "keys": draw_keys(jax.random.fold_in(splits[6], 71), 0),
        "values": noise(splits[2], (SECTIONS, FRAMES, HEIGHT, WIDTH, CHANNELS), 1.0, 6.0, ((0, 2), (2, 4), (3, 4))),
        "cotangent": noise(splits[3], (SECTIONS, FRAMES, HEIGHT, WIDTH, CHANNELS), 1.0, 6.0, ((0, 2), (2, 4), (3, 4))),
        "upstream": noise(splits[4], (SECTIONS, FRAMES, HEIGHT, WIDTH, CHANNELS), 1.0, 6.0, ((0, 2), (2, 4), (3, 4))),
        "block_mask": draw_block_mask(jax.random.fold_in(splits[6], 71), 0),
    }


def window_live(mask_table, tile_row, tile_col, grid_height, grid_width):
    box_span = 3 * TILE
    offsets = jnp.arange(box_span, dtype=jnp.int32)
    rows_at = tile_row * TILE - TILE + offsets
    cols_at = tile_col * TILE - TILE + offsets
    part_of = offsets // TILE
    thirds = jnp.arange(3, dtype=jnp.int32)
    part_hot = (part_of[:, None] == thirds[None, :]).astype(jnp.float32)
    grid_mask = mask_table.reshape(3, 3).astype(jnp.float32)
    allowed = jnp.dot(jnp.dot(part_hot, grid_mask), part_hot.T)
    inside_rows = (rows_at >= 0) & (rows_at < grid_height)
    inside_cols = (cols_at >= 0) & (cols_at < grid_width)
    return (allowed > 0.5) & inside_rows[:, None] & inside_cols[None, :]


def tile_grads(query_rows, key_rows, value_rows, grad_rows, live_keys):
    inv_root = HEAD_DIM ** -0.5
    query_wide = query_rows.astype(jnp.float32)
    key_wide = key_rows.astype(jnp.float32)
    value_wide = value_rows.astype(jnp.float32)
    grad_wide = grad_rows.astype(jnp.float32)
    scores = jnp.einsum("qhd,khd->hqk", query_wide, key_wide) * inv_root
    scores = jnp.where(live_keys[None, None, :], scores, -jnp.inf)
    row_max = jnp.max(scores, axis=2, keepdims=True)
    weights = jnp.exp(scores - row_max)
    softmax_probs = weights / jnp.sum(weights, axis=2, keepdims=True)
    probs_low = softmax_probs.astype(jnp.bfloat16)
    probs_wide = probs_low.astype(jnp.float32)
    attended = jnp.einsum("hqk,khd->qhd", probs_wide, value_wide)
    deltas = jnp.sum(grad_wide * attended, axis=2)
    grad_probs = jnp.einsum("qhd,khd->hqk", grad_wide, value_wide)
    grad_scores = (softmax_probs * (grad_probs - deltas.T[:, :, None]) * inv_root).astype(jnp.bfloat16)
    scores_wide = grad_scores.astype(jnp.float32)
    grad_query = jnp.einsum("hqk,khd->qhd", scores_wide, key_wide)
    grad_key = jnp.einsum("hqk,qhd->khd", scores_wide, query_wide)
    grad_value = jnp.einsum("hqk,qhd->khd", probs_wide, grad_wide)
    return grad_query, grad_key, grad_value


def rounded(values_in):
    low = lax.optimization_barrier(values_in.astype(jnp.bfloat16))
    return low.astype(jnp.float32)


def section_grads(section_queries, section_keys, section_values, section_grad, section_mask):
    frames_n, grid_height, grid_width, chan_count = section_queries.shape
    box_span = 3 * TILE
    own_width = SPAN_TILES * TILE
    ext_width = own_width + 2 * TILE
    pair_rows_n = grid_height // TILE
    pair_cols_n = grid_width // own_width
    tile_tokens = frames_n * TILE * TILE
    box_rows = frames_n * box_span * box_span
    padded_kv = jnp.pad(jnp.concatenate((section_keys, section_values), axis=3), ((0, 0), (TILE, TILE), (TILE, TILE), (0, 0)))
    zero_idx = jnp.int32(0)

    def one_pair(pair_index):
        pair_row = (pair_index // pair_cols_n).astype(jnp.int32)
        pair_col = (pair_index % pair_cols_n).astype(jnp.int32)
        start_row = (pair_row * TILE).astype(jnp.int32)
        start_col = (pair_col * own_width).astype(jnp.int32)
        region = lax.dynamic_slice(padded_kv, (zero_idx, start_row, start_col, zero_idx), (frames_n, box_span, ext_width, 2 * chan_count))
        query_block = lax.dynamic_slice(section_queries, (zero_idx, start_row, start_col, zero_idx), (frames_n, TILE, own_width, chan_count))
        grad_block = lax.dynamic_slice(section_grad, (zero_idx, start_row, start_col, zero_idx), (frames_n, TILE, own_width, chan_count))
        ext_grads = jnp.zeros((frames_n, box_span, ext_width, 2 * chan_count), jnp.float32)
        query_parts = []
        for tile_at in range(SPAN_TILES):
            tile_col = (pair_col * SPAN_TILES + tile_at).astype(jnp.int32)
            mask_row = lax.dynamic_slice(section_mask, (pair_row, tile_col, zero_idx), (1, 1, 9)).reshape(9)
            live_cells = window_live(mask_row, pair_row, tile_col, grid_height, grid_width)
            live_keys = jnp.broadcast_to(live_cells[None], (frames_n, box_span, box_span)).reshape(box_rows)
            start = tile_at * TILE
            box_tile = region[:, :, start:start + box_span, :]
            grad_query, grad_key, grad_value = tile_grads(
                query_block[:, :, start:start + TILE, :].reshape(tile_tokens, HEADS, HEAD_DIM),
                box_tile[..., :chan_count].reshape(box_rows, HEADS, HEAD_DIM),
                box_tile[..., chan_count:].reshape(box_rows, HEADS, HEAD_DIM),
                grad_block[:, :, start:start + TILE, :].reshape(tile_tokens, HEADS, HEAD_DIM),
                live_keys)
            box_grads = jnp.concatenate((grad_key.reshape(frames_n, box_span, box_span, chan_count),
                                         grad_value.reshape(frames_n, box_span, box_span, chan_count)), axis=3)
            ext_grads = ext_grads.at[:, :, start:start + box_span, :].add(box_grads)
            query_parts.append(grad_query.reshape(frames_n, TILE, TILE, chan_count).astype(jnp.bfloat16))
        center = ext_grads[:, :, TILE:ext_width - TILE, :]
        rims = jnp.concatenate([ext_grads[:, :, :TILE, :], ext_grads[:, :, ext_width - TILE:, :]], axis=2).astype(jnp.bfloat16)
        return jnp.concatenate(query_parts, axis=2), center, rims

    query_pairs, centers, rims = lax.map(one_pair, jnp.arange(pair_rows_n * pair_cols_n, dtype=jnp.int32))
    centers = centers.reshape(pair_rows_n, pair_cols_n, frames_n, box_span, own_width, 2 * chan_count)
    rims = rims.reshape(pair_rows_n, pair_cols_n, frames_n, box_span, 2 * TILE, 2 * chan_count).astype(jnp.float32)
    left_parts = rims[..., :TILE, :]
    right_parts = rims[..., TILE:, :]
    col_zero = jnp.zeros_like(right_parts[:, :1])
    from_before = jnp.concatenate([col_zero, right_parts[:, :pair_cols_n - 1]], axis=1)
    from_after = jnp.concatenate([left_parts[:, 1:], col_zero], axis=1)
    gap_shape = list(from_before.shape)
    gap_shape[4] = own_width - 2 * TILE
    col_gap = jnp.zeros(gap_shape, jnp.float32)
    col_folded = centers + jnp.concatenate([from_before, col_gap, from_after], axis=4)
    lower = rounded(col_folded[:, :, :, :TILE])
    upper = rounded(col_folded[:, :, :, 2 * TILE:])
    row_zero = jnp.zeros_like(lower[:1])
    from_above = jnp.concatenate([row_zero, upper[:pair_rows_n - 1]], axis=0)
    from_below = jnp.concatenate([lower[1:], row_zero], axis=0)
    folded_all = (col_folded[:, :, :, TILE:2 * TILE] + from_above + from_below).astype(jnp.bfloat16)
    folded_all = folded_all.transpose(2, 0, 3, 1, 4, 5).reshape(frames_n, grid_height, grid_width, 2 * chan_count)
    query_pairs = query_pairs.reshape(pair_rows_n, pair_cols_n, frames_n, TILE, own_width, chan_count)
    query_grid = query_pairs.transpose(2, 0, 3, 1, 4, 5).reshape(frames_n, grid_height, grid_width, chan_count)
    return query_grid, folded_all[..., :chan_count], folded_all[..., chan_count:]


def reference(queries, keys, values, cotangent, upstream, block_mask):
    handed = jnp.concatenate([upstream[1:], jnp.zeros_like(upstream[:1])], axis=0)
    grad_out = (cotangent.astype(jnp.float32) + handed.astype(jnp.float32)).astype(jnp.bfloat16)

    def per_section(slices):
        return section_grads(slices[0], slices[1], slices[2], slices[3], slices[4])

    grad_queries, grad_keys, grad_values = lax.map(per_section, (queries, keys, values, grad_out, block_mask))
    return (grad_queries, grad_keys, grad_values)
```

```python
import functools

import jax
import jax.numpy as jnp
from jax import lax
from jax.experimental import pallas as pl
from jax.experimental.pallas import tpu as pltpu
from jax.sharding import PartitionSpec as P

HEADS = 12
HEAD_DIM = 128
TILE = 8


def passed_along(value, axis, steps):
    count = lax.axis_size(axis)
    initial, last = (max(0, -steps), min(count, count - steps))
    return lax.ppermute(value, axis, [(source, source + steps) for source in range(initial, last)])


def extended(value, sides, width):
    for axis, dim in sides:
        size, length = (lax.axis_size(axis), value.shape[dim])
        up = [(i, (i + 1) % size) for i in range(size - 1)]
        down = [(j, i) for i, j in up]
        last = lax.slice_in_dim(value, length - width, length, axis=dim)
        initial = lax.slice_in_dim(value, 0, width, axis=dim)
        before = lax.ppermute(last, axis, up)
        after = lax.ppermute(initial, axis, down)
        value = jnp.concatenate([before, value, after], axis=dim)
    return value


def window_live(mask_table, tile_row, tile_col, grid_height, grid_width):
    box_span = 3 * TILE
    offsets = jnp.arange(box_span, dtype=jnp.int32)
    rows_at = tile_row * TILE - TILE + offsets
    cols_at = tile_col * TILE - TILE + offsets
    part_of = offsets // TILE
    thirds = jnp.arange(3, dtype=jnp.int32)
    part_hot = (part_of[:, None] == thirds[None, :]).astype(jnp.float32)
    grid_mask = mask_table.reshape(3, 3).astype(jnp.float32)
    allowed = jnp.dot(jnp.dot(part_hot, grid_mask), part_hot.T)
    inside_rows = (rows_at >= 0) & (rows_at < grid_height)
    inside_cols = (cols_at >= 0) & (cols_at < grid_width)
    return (allowed > 0.5) & inside_rows[:, None] & inside_cols[None, :]


def body(queries, keys, values, cotangent, upstream, block_mask):
    handed = passed_along(upstream, "section", -1)
    paired = jnp.stack((keys, values), axis=0)
    box_kv = extended(paired, (("ha", 3), ("wa", 4)), TILE)
    grad_out = (cotangent.astype(jnp.float32) + handed.astype(jnp.float32)).astype(jnp.bfloat16)
    frames_n = queries.shape[1]
    chan_count = queries.shape[4]
    own_width = queries.shape[3]
    span_count = own_width // TILE
    box_span = 3 * TILE
    ext_width = own_width + 2 * TILE
    query_count = frames_n * TILE * own_width
    region_rows = frames_n * box_span * ext_width
    grid_height = TILE * lax.axis_size("ha")
    grid_width = own_width * lax.axis_size("wa")
    tile_row = lax.axis_index("ha")
    inv_root = HEAD_DIM ** (-0.5)
    region_live = []
    for tile_at in range(span_count):
        tile_col = lax.axis_index("wa") * span_count + tile_at
        live_cells = window_live(
            block_mask[0, 0, tile_at], tile_row, tile_col, grid_height, grid_width
        )
        placed = jnp.pad(
            live_cells, ((0, 0), (tile_at * TILE, ext_width - box_span - tile_at * TILE))
        )
        region_live.append(placed[None].reshape(region_rows))
    live_table = jnp.stack(region_live, axis=0).astype(jnp.float32)
    col_tile = jnp.arange(own_width, dtype=jnp.int32) // TILE
    query_tile = jnp.broadcast_to(col_tile[None, None, :], (frames_n, TILE, own_width)).reshape(
        query_count
    )
    tile_hot = (query_tile[:, None] == jnp.arange(span_count, dtype=jnp.int32)[None, :]).astype(
        jnp.float32
    )
    live_pairs = jnp.dot(tile_hot, live_table) > 0.5
    query_rows = queries[0].reshape(query_count, HEADS, HEAD_DIM)
    grad_rows = grad_out[0].reshape(query_count, HEADS, HEAD_DIM)
    key_rows = box_kv[0, 0].reshape(region_rows, HEADS, HEAD_DIM)
    value_rows = box_kv[1, 0].reshape(region_rows, HEADS, HEAD_DIM)
    scores = (
        jnp.einsum("qhd,khd->hqk", query_rows, key_rows, preferred_element_type=jnp.float32)
        * inv_root
    )
    scores = jnp.where(live_pairs[None], scores, -jnp.inf)
    row_max = jnp.max(scores, axis=2, keepdims=True)
    weights = jnp.exp(scores - row_max)
    softmax_probs = weights / jnp.sum(weights, axis=2, keepdims=True)
    probs_low = softmax_probs.astype(jnp.bfloat16)
    attended = jnp.einsum("hqk,khd->qhd", probs_low, value_rows, preferred_element_type=jnp.float32)
    deltas = jnp.sum(grad_rows.astype(jnp.float32) * attended, axis=2)
    grad_probs = jnp.einsum(
        "qhd,khd->hqk", grad_rows, value_rows, preferred_element_type=jnp.float32
    )
    grad_scores = (softmax_probs * (grad_probs - deltas.T[:, :, None]) * inv_root).astype(
        jnp.bfloat16
    )
    grad_query = jnp.einsum(
        "hqk,khd->qhd", grad_scores, key_rows, preferred_element_type=jnp.float32
    )
    grad_queries = grad_query.reshape(1, frames_n, TILE, own_width, chan_count).astype(jnp.bfloat16)
    weight_pair = jnp.stack((grad_scores, probs_low), axis=0)
    source_pair = jnp.stack((query_rows, grad_rows), axis=1)
    region_grads = jnp.einsum(
        "shqk,qshd->skhd", weight_pair, source_pair, preferred_element_type=jnp.float32
    )
    region_grads = region_grads.reshape(2, frames_n, box_span, ext_width, chan_count)
    col_send = jnp.concatenate(
        [region_grads[:, :, :, :TILE], region_grads[:, :, :, ext_width - TILE :]], axis=3
    ).astype(jnp.bfloat16)
    col_back = extended(col_send[None], (("wa", 4),), TILE)[0]
    back_width = col_back.shape[3]
    gap_shape = list(col_back.shape)
    gap_shape[3] = own_width - 2 * TILE
    col_gap = jnp.zeros(gap_shape, jnp.float32)
    col_folded = region_grads[:, :, :, TILE : ext_width - TILE] + jnp.concatenate(
        [
            col_back[:, :, :, :TILE].astype(jnp.float32),
            col_gap,
            col_back[:, :, :, back_width - TILE :].astype(jnp.float32),
        ],
        axis=3,
    )
    row_send = jnp.concatenate(
        [col_folded[:, :, :TILE], col_folded[:, :, 2 * TILE :]], axis=2
    ).astype(jnp.bfloat16)
    row_back = extended(row_send[None], (("ha", 3),), TILE)[0]
    folded_all = (
        col_folded[:, :, TILE : 2 * TILE]
        + row_back[:, :, :TILE].astype(jnp.float32)
        + row_back[:, :, 3 * TILE :].astype(jnp.float32)
    ).astype(jnp.bfloat16)
    grad_keys = folded_all[0][None]
    grad_values = folded_all[1][None]
    return (grad_queries, grad_keys, grad_values)


NEG = -1e30
LANES = 128
MESH_ID = pl.DeviceIdType.MESH


def to_tiles(block):
    return jnp.concatenate(
        [block[r * 16 + t * 8 : r * 16 + t * 8 + 8] for t in range(2) for r in range(8)], axis=0
    )


def from_tiles(block):
    return jnp.concatenate(
        [block[t * 64 + r * 8 : t * 64 + r * 8 + 8] for r in range(8) for t in range(2)], axis=0
    )


def fused_kernel(
    sections, rows_n, cols_n,
    q_ref, k_ref, v_ref, c_ref, u_ref, mask_ref,
    oq_ref, ok_ref, ov_ref,
    handed, kv_send, qg_send, bias_send, kv_buf, qg_buf, bias_buf, acc,
    dz_send, dz_recv, dq_send, dq_recv, dkv_send, dkv_recv,
    sec_sem, kv_sem, qg_sem, bias_sem, z_sem, dz_sem, dq_sem, dkv_sem,
):
    f32, bf16 = jnp.float32, jnp.bfloat16
    sec = lax.axis_index("section")
    row = lax.axis_index("ha")
    col = lax.axis_index("wa")
    own_heads = HEADS // cols_n
    tiles = 2 * cols_n
    peers = [lax.rem(col + j, cols_n) for j in range(1, cols_n)]
    has_up, has_down = row > 0, row < rows_n - 1
    inv_root = HEAD_DIM ** (-0.5)
    scale = inv_root * 1.4426950408889634

    barrier = pltpu.get_barrier_semaphore()
    for peer in peers:
        pl.semaphore_signal(barrier, inc=1, device_id={"wa": peer}, device_id_type=MESH_ID)
    for cond, dev in (
        (has_up, {"ha": row - 1}),
        (has_down, {"ha": row + 1}),
        (sec > 0, {"section": sec - 1}),
        (sec < sections - 1, {"section": sec + 1}),
    ):
        @pl.when(cond)
        def _(dev=dev):
            pl.semaphore_signal(barrier, inc=1, device_id=dev, device_id_type=MESH_ID)

    def remote(src, dst, sems, at, dev):
        return pltpu.make_async_remote_copy(
            src_ref=src, dst_ref=dst, send_sem=sems.at[(0, *at)], recv_sem=sems.at[(1, *at)],
            device_id=dev, device_id_type=MESH_ID,
        )

    sec_copy = remote(u_ref, handed, sec_sem, (), {"section": sec - 1})

    def kv_copy(h, j):
        peer = peers[j]
        return remote(
            kv_send.at[peer * own_heads + h],
            kv_buf.at[h, 1, :, pl.ds(1 + 2 * col, 2)],
            kv_sem, (h, j), {"wa": peer},
        )

    def qg_copy(h, j):
        peer = peers[j]
        return remote(
            qg_send.at[peer * own_heads + h], qg_buf.at[h, col], qg_sem, (h, j), {"wa": peer}
        )

    def bias_copy(j):
        return remote(bias_send, bias_buf.at[col], bias_sem, (j,), {"wa": peers[j]})

    def z_copy(h, d):
        return remote(
            kv_buf.at[h, 1, :, pl.ds(1, tiles)],
            kv_buf.at[h, 2 - 2 * d, :, pl.ds(1, tiles)],
            z_sem, (h, d), {"ha": row - 1 + 2 * d},
        )

    def dz_copy(h, d):
        return remote(
            dz_send.at[h, d], dz_recv.at[h, d], dz_sem, (h, d), {"ha": row - 1 + 2 * d}
        )

    def dq_copy(h, j):
        peer = peers[j]
        return remote(
            dq_send.at[h, peer], dq_recv.at[col * own_heads + h], dq_sem, (h, j), {"wa": peer}
        )

    def dkv_copy(h, j):
        peer = peers[j]
        return remote(
            dkv_send.at[h, peer], dkv_recv.at[col * own_heads + h], dkv_sem, (h, j), {"wa": peer}
        )

    def head_cols(head):
        return pl.ds(pl.multiple_of(head * LANES, LANES), LANES)

    total = (
        cols_n - 1
        + has_up.astype(jnp.int32) + has_down.astype(jnp.int32)
        + (sec > 0).astype(jnp.int32) + (sec < sections - 1).astype(jnp.int32)
    )
    pl.semaphore_wait(barrier, total)

    @pl.when(sec > 0)
    def _():
        sec_copy.start()

    @pl.loop(0, HEADS)
    def _(head):
        at = head_cols(head)
        kv_send[head, 0] = to_tiles(k_ref[:, at].astype(f32)).astype(bf16).reshape(2, 64, LANES)
        kv_send[head, 1] = to_tiles(v_ref[:, at].astype(f32)).astype(bf16).reshape(2, 64, LANES)

    for h in range(own_heads):
        for j in range(cols_n - 1):
            kv_copy(h, j).start()

    lane = lax.broadcasted_iota(jnp.int32, (1, LANES), 1)
    bias_send[...] = jnp.full(bias_send.shape, NEG, f32)
    for i in range(3):
        row_in = (row + (i - 1) >= 0) & (row + (i - 1) < rows_n)
        for jj in range(4):
            tile = 2 * col + (jj - 1)
            inside = row_in & (tile >= 0) & (tile < tiles)
            first = mask_ref[0, 3 * i + jj] if jj < 3 else jnp.int32(0)
            second = mask_ref[1, 3 * i + jj - 1] if jj > 0 else jnp.int32(0)
            seen = jnp.where(lane < 64, first, second) * inside.astype(jnp.int32)
            bias_send[pl.ds(4 * i + jj, 1), :] = jnp.where(seen > 0, 0.0, NEG).astype(f32)
    for j in range(cols_n - 1):
        bias_copy(j).start()
    bias_buf[col] = bias_send[...]

    zero_tile = jnp.zeros((2, 64, LANES), bf16)
    for h in range(own_heads):
        kv_buf[h, 1, :, pl.ds(1 + 2 * col, 2)] = kv_send[col * own_heads + h]
        for i in range(3):
            kv_buf[h, i, :, 0] = zero_tile
            kv_buf[h, i, :, tiles + 1] = zero_tile

    for cond, i in ((row == 0, 0), (row == rows_n - 1, 2)):
        @pl.when(cond)
        def _(i=i):
            for h in range(own_heads):
                @pl.loop(0, tiles)
                def _(t, h=h):
                    kv_buf[h, i, :, t + 1] = zero_tile

    @pl.when(sec == sections - 1)
    def _():
        handed[...] = jnp.zeros_like(handed)

    @pl.when(sec < sections - 1)
    def _():
        sec_copy.wait_recv()

    @pl.loop(0, HEADS)
    def _(head):
        at = head_cols(head)
        qg_send[head, 0] = to_tiles(q_ref[:, at].astype(f32)).astype(bf16)
        grad = c_ref[:, at].astype(f32) + handed[:, at].astype(f32)
        qg_send[head, 1] = to_tiles(grad).astype(bf16)

    for h in range(own_heads):
        for j in range(cols_n - 1):
            qg_copy(h, j).start()
        qg_buf[h, col] = qg_send[col * own_heads + h]

    for h in range(own_heads):
        for j in range(cols_n - 1):
            kv_copy(h, j).wait_recv()

        @pl.when(has_up)
        def _(h=h):
            z_copy(h, 0).start()

        @pl.when(has_down)
        def _(h=h):
            z_copy(h, 1).start()

    for j in range(cols_n - 1):
        bias_copy(j).wait_recv()

    nt = (((1,), (1,)), ((), ()))
    tn = (((0,), (0,)), ((), ()))

    def dot(a, b, dims):
        return lax.dot_general(a, b, dims, preferred_element_type=f32)

    def compute(h):
        acc[h] = jnp.zeros(acc.shape[1:], f32)

        @pl.loop(0, cols_n)
        def _(pair):
            query = qg_buf[h, pair, 0]
            grad = qg_buf[h, pair, 1]
            box = pl.ds(2 * pair, 4)
            key_rows = [kv_buf[h, i, 0, box].reshape(256, LANES) for i in range(3)]
            value_rows = [kv_buf[h, i, 1, box].reshape(256, LANES) for i in range(3)]
            blocks = []
            for i in range(3):
                part = dot(key_rows[i], query, nt) * scale
                for jj in range(4):
                    blocks.append(
                        part[jj * 64 : jj * 64 + 64] + bias_buf[pair, pl.ds(4 * i + jj, 1), :]
                    )
            scores = jnp.concatenate(blocks, axis=0)
            weights = jnp.exp2(scores - jnp.max(scores, axis=0, keepdims=True))
            probs = weights * (1.0 / jnp.sum(weights, axis=0, keepdims=True))
            low = probs.astype(bf16)
            grad_probs = jnp.concatenate([dot(rows, grad, nt) for rows in value_rows], axis=0)
            deltas = jnp.sum(low.astype(f32) * grad_probs, axis=0, keepdims=True)
            grad_scores = (probs * (grad_probs - deltas) * inv_root).astype(bf16)
            keys_all = jnp.concatenate(key_rows, axis=0)
            dq_send[h, pair] = dot(grad_scores, keys_all, tn).astype(bf16)
            grad_key = dot(grad_scores, query, (((1,), (0,)), ((), ())))
            grad_value = dot(low, grad, (((1,), (0,)), ((), ())))
            for i in range(3):
                at = slice(i * 256, i * 256 + 256)
                acc[h, i, 0, box] += grad_key[at].reshape(4, 64, LANES)
                acc[h, i, 1, box] += grad_value[at].reshape(4, 64, LANES)

    def finish(h):
        @pl.when(has_down)
        def _():
            dz_copy(h, 0).wait_recv()

        @pl.when(has_up)
        def _():
            dz_copy(h, 1).wait_recv()

        for cond, d in ((jnp.logical_not(has_down), 0), (jnp.logical_not(has_up), 1)):
            @pl.when(cond)
            def _(d=d):
                dz_recv[h, d] = jnp.zeros(dz_recv.shape[2:], bf16)

        @pl.loop(0, cols_n)
        def _(pair):
            for kv in range(2):
                total = (
                    acc[h, 1, kv, pl.ds(1 + 2 * pair, 2)]
                    + dz_recv[h, 0, kv, pl.ds(2 * pair, 2)].astype(f32)
                    + dz_recv[h, 1, kv, pl.ds(2 * pair, 2)].astype(f32)
                )
                dkv_send[h, pair, kv] = total.astype(bf16).reshape(128, LANES)

        for j in range(cols_n - 1):
            dkv_copy(h, j).start()
        dkv_recv[col * own_heads + h] = dkv_send[h, col]

    for h in range(own_heads):
        for j in range(cols_n - 1):
            qg_copy(h, j).wait_recv()

        @pl.when(has_down)
        def _(h=h):
            z_copy(h, 0).wait_recv()

        @pl.when(has_up)
        def _(h=h):
            z_copy(h, 1).wait_recv()

        compute(h)
        for d, cond in ((0, has_up), (1, has_down)):
            @pl.when(cond)
            def _(d=d, h=h):
                for kv in range(2):
                    dz_send[h, d, kv] = acc[h, 2 * d, kv, pl.ds(1, tiles)].astype(bf16)
                dz_copy(h, d).start()
        for j in range(cols_n - 1):
            dq_copy(h, j).start()
        dq_recv[col * own_heads + h] = dq_send[h, col]
        if h > 0:
            finish(h - 1)
    finish(own_heads - 1)

    for h in range(own_heads):
        for j in range(cols_n - 1):
            dq_copy(h, j).wait_recv()

    @pl.loop(0, HEADS)
    def _(head):
        oq_ref[:, head_cols(head)] = from_tiles(dq_recv[head].astype(f32)).astype(bf16)

    for h in range(own_heads):
        for j in range(cols_n - 1):
            dkv_copy(h, j).wait_recv()

    @pl.loop(0, HEADS)
    def _(head):
        ok_ref[:, head_cols(head)] = from_tiles(dkv_recv[head, 0].astype(f32)).astype(bf16)
        ov_ref[:, head_cols(head)] = from_tiles(dkv_recv[head, 1].astype(f32)).astype(bf16)

    @pl.when(sec > 0)
    def _():
        sec_copy.wait_send()

    for j in range(cols_n - 1):
        bias_copy(j).wait_send()
        for h in range(own_heads):
            for copy in (kv_copy, qg_copy, dq_copy, dkv_copy):
                copy(h, j).wait_send()
    for d, cond in ((0, has_up), (1, has_down)):
        @pl.when(cond)
        def _(d=d):
            for h in range(own_heads):
                z_copy(h, d).wait_send()
                dz_copy(h, d).wait_send()


def fused_body(queries, keys, values, cotangent, upstream, block_mask):
    sections, rows_n, cols_n = (lax.axis_size(a) for a in ("section", "ha", "wa"))
    shape = queries.shape
    tokens = shape[1] * shape[2] * shape[3]
    flat = (tokens, shape[4])
    own = HEADS // cols_n
    tiles = 2 * cols_n
    bf16, f32 = jnp.bfloat16, jnp.float32
    vmem = pl.BlockSpec(memory_space=pltpu.VMEM)
    dma = pltpu.SemaphoreType.DMA
    out = pl.pallas_call(
        functools.partial(fused_kernel, sections, rows_n, cols_n),
        out_shape=[jax.ShapeDtypeStruct(flat, bf16)] * 3,
        in_specs=[vmem] * 5 + [pl.BlockSpec(memory_space=pltpu.SMEM)],
        out_specs=[vmem] * 3,
        scratch_shapes=[
            pltpu.VMEM(flat, bf16),
            pltpu.VMEM((HEADS, 2, 2, 64, LANES), bf16),
            pltpu.VMEM((HEADS, 2, 128, LANES), bf16),
            pltpu.VMEM((16, LANES), f32),
            pltpu.VMEM((own, 3, 2, tiles + 2, 64, LANES), bf16),
            pltpu.VMEM((own, cols_n, 2, 128, LANES), bf16),
            pltpu.VMEM((cols_n, 16, LANES), f32),
            pltpu.VMEM((own, 3, 2, tiles + 2, 64, LANES), f32),
            pltpu.VMEM((own, 2, 2, tiles, 64, LANES), bf16),
            pltpu.VMEM((own, 2, 2, tiles, 64, LANES), bf16),
            pltpu.VMEM((own, cols_n, 128, LANES), bf16),
            pltpu.VMEM((HEADS, 128, LANES), bf16),
            pltpu.VMEM((own, cols_n, 2, 128, LANES), bf16),
            pltpu.VMEM((HEADS, 2, 128, LANES), bf16),
            dma((2,)),
            dma((2, own, cols_n - 1)),
            dma((2, own, cols_n - 1)),
            dma((2, cols_n - 1)),
            dma((2, own, 2)),
            dma((2, own, 2)),
            dma((2, own, cols_n - 1)),
            dma((2, own, cols_n - 1)),
        ],
        compiler_params=pltpu.CompilerParams(
            collective_id=0, has_side_effects=True, vmem_limit_bytes=50 * 2**20
        ),
    )(
        queries.reshape(flat), keys.reshape(flat), values.reshape(flat),
        cotangent.reshape(flat), upstream.reshape(flat), block_mask.reshape(2, 9),
    )
    return tuple(x.reshape(shape) for x in out)


def solution(mesh):
    fits = mesh.shape["wa"] == 4
    return jax.shard_map(
        fused_body if fits else body,
        mesh=mesh,
        in_specs=(
            P("section", None, "ha", "wa", None),
            P("section", None, "ha", "wa", None),
            P("section", None, "ha", "wa", None),
            P("section", None, "ha", "wa", None),
            P("section", None, "ha", "wa", None),
            P("section", "ha", "wa", None),
        ),
        out_specs=(
            P("section", None, "ha", "wa", None),
            P("section", None, "ha", "wa", None),
            P("section", None, "ha", "wa", None),
        ),
        check_vma=False,
    )
```

```python
import functools

import jax
import jax.numpy as jnp
from jax import lax
from jax.experimental import pallas as pl
from jax.experimental.pallas import tpu as pltpu
from jax.sharding import PartitionSpec as P

HEADS = 12
HEAD_DIM = 128
TILE = 8


def passed_along(value, axis, steps):
    count = lax.axis_size(axis)
    initial, last = (max(0, -steps), min(count, count - steps))
    return lax.ppermute(value, axis, [(source, source + steps) for source in range(initial, last)])


def extended(value, sides, width):
    for axis, dim in sides:
        size, length = (lax.axis_size(axis), value.shape[dim])
        up = [(i, (i + 1) % size) for i in range(size - 1)]
        down = [(j, i) for i, j in up]
        last = lax.slice_in_dim(value, length - width, length, axis=dim)
        initial = lax.slice_in_dim(value, 0, width, axis=dim)
        before = lax.ppermute(last, axis, up)
        after = lax.ppermute(initial, axis, down)
        value = jnp.concatenate([before, value, after], axis=dim)
    return value


def window_live(mask_table, tile_row, tile_col, grid_height, grid_width):
    box_span = 3 * TILE
    offsets = jnp.arange(box_span, dtype=jnp.int32)
    rows_at = tile_row * TILE - TILE + offsets
    cols_at = tile_col * TILE - TILE + offsets
    part_of = offsets // TILE
    thirds = jnp.arange(3, dtype=jnp.int32)
    part_hot = (part_of[:, None] == thirds[None, :]).astype(jnp.float32)
    grid_mask = mask_table.reshape(3, 3).astype(jnp.float32)
    allowed = jnp.dot(jnp.dot(part_hot, grid_mask), part_hot.T)
    inside_rows = (rows_at >= 0) & (rows_at < grid_height)
    inside_cols = (cols_at >= 0) & (cols_at < grid_width)
    return (allowed > 0.5) & inside_rows[:, None] & inside_cols[None, :]


def body(queries, keys, values, cotangent, upstream, block_mask):
    handed = passed_along(upstream, "section", -1)
    paired = jnp.stack((keys, values), axis=0)
    box_kv = extended(paired, (("ha", 3), ("wa", 4)), TILE)
    grad_out = (cotangent.astype(jnp.float32) + handed.astype(jnp.float32)).astype(jnp.bfloat16)
    frames_n = queries.shape[1]
    chan_count = queries.shape[4]
    own_width = queries.shape[3]
    span_count = own_width // TILE
    box_span = 3 * TILE
    ext_width = own_width + 2 * TILE
    query_count = frames_n * TILE * own_width
    region_rows = frames_n * box_span * ext_width
    grid_height = TILE * lax.axis_size("ha")
    grid_width = own_width * lax.axis_size("wa")
    tile_row = lax.axis_index("ha")
    inv_root = HEAD_DIM ** (-0.5)
    region_live = []
    for tile_at in range(span_count):
        tile_col = lax.axis_index("wa") * span_count + tile_at
        live_cells = window_live(
            block_mask[0, 0, tile_at], tile_row, tile_col, grid_height, grid_width
        )
        placed = jnp.pad(
            live_cells, ((0, 0), (tile_at * TILE, ext_width - box_span - tile_at * TILE))
        )
        region_live.append(placed[None].reshape(region_rows))
    live_table = jnp.stack(region_live, axis=0).astype(jnp.float32)
    col_tile = jnp.arange(own_width, dtype=jnp.int32) // TILE
    query_tile = jnp.broadcast_to(col_tile[None, None, :], (frames_n, TILE, own_width)).reshape(
        query_count
    )
    tile_hot = (query_tile[:, None] == jnp.arange(span_count, dtype=jnp.int32)[None, :]).astype(
        jnp.float32
    )
    live_pairs = jnp.dot(tile_hot, live_table) > 0.5
    query_rows = queries[0].reshape(query_count, HEADS, HEAD_DIM)
    grad_rows = grad_out[0].reshape(query_count, HEADS, HEAD_DIM)
    key_rows = box_kv[0, 0].reshape(region_rows, HEADS, HEAD_DIM)
    value_rows = box_kv[1, 0].reshape(region_rows, HEADS, HEAD_DIM)
    scores = (
        jnp.einsum("qhd,khd->hqk", query_rows, key_rows, preferred_element_type=jnp.float32)
        * inv_root
    )
    scores = jnp.where(live_pairs[None], scores, -jnp.inf)
    row_max = jnp.max(scores, axis=2, keepdims=True)
    weights = jnp.exp(scores - row_max)
    softmax_probs = weights / jnp.sum(weights, axis=2, keepdims=True)
    probs_low = softmax_probs.astype(jnp.bfloat16)
    attended = jnp.einsum("hqk,khd->qhd", probs_low, value_rows, preferred_element_type=jnp.float32)
    deltas = jnp.sum(grad_rows.astype(jnp.float32) * attended, axis=2)
    grad_probs = jnp.einsum(
        "qhd,khd->hqk", grad_rows, value_rows, preferred_element_type=jnp.float32
    )
    grad_scores = (softmax_probs * (grad_probs - deltas.T[:, :, None]) * inv_root).astype(
        jnp.bfloat16
    )
    grad_query = jnp.einsum(
        "hqk,khd->qhd", grad_scores, key_rows, preferred_element_type=jnp.float32
    )
    grad_queries = grad_query.reshape(1, frames_n, TILE, own_width, chan_count).astype(jnp.bfloat16)
    weight_pair = jnp.stack((grad_scores, probs_low), axis=0)
    source_pair = jnp.stack((query_rows, grad_rows), axis=1)
    region_grads = jnp.einsum(
        "shqk,qshd->skhd", weight_pair, source_pair, preferred_element_type=jnp.float32
    )
    region_grads = region_grads.reshape(2, frames_n, box_span, ext_width, chan_count)
    col_send = jnp.concatenate(
        [region_grads[:, :, :, :TILE], region_grads[:, :, :, ext_width - TILE :]], axis=3
    ).astype(jnp.bfloat16)
    col_back = extended(col_send[None], (("wa", 4),), TILE)[0]
    back_width = col_back.shape[3]
    gap_shape = list(col_back.shape)
    gap_shape[3] = own_width - 2 * TILE
    col_gap = jnp.zeros(gap_shape, jnp.float32)
    col_folded = region_grads[:, :, :, TILE : ext_width - TILE] + jnp.concatenate(
        [
            col_back[:, :, :, :TILE].astype(jnp.float32),
            col_gap,
            col_back[:, :, :, back_width - TILE :].astype(jnp.float32),
        ],
        axis=3,
    )
    row_send = jnp.concatenate(
        [col_folded[:, :, :TILE], col_folded[:, :, 2 * TILE :]], axis=2
    ).astype(jnp.bfloat16)
    row_back = extended(row_send[None], (("ha", 3),), TILE)[0]
    folded_all = (
        col_folded[:, :, TILE : 2 * TILE]
        + row_back[:, :, :TILE].astype(jnp.float32)
        + row_back[:, :, 3 * TILE :].astype(jnp.float32)
    ).astype(jnp.bfloat16)
    grad_keys = folded_all[0][None]
    grad_values = folded_all[1][None]
    return (grad_queries, grad_keys, grad_values)


NEG = -1e30
LANES = 128
MESH_ID = pl.DeviceIdType.MESH


def to_tiles(block):
    return jnp.concatenate(
        [block[r * 16 + t * 8 : r * 16 + t * 8 + 8] for t in range(2) for r in range(8)], axis=0
    )


def from_tiles(block):
    return jnp.concatenate(
        [block[t * 64 + r * 8 : t * 64 + r * 8 + 8] for r in range(8) for t in range(2)], axis=0
    )


def fused_kernel(
    sections, rows_n, cols_n,
    q_hbm, k_hbm, v_hbm, c_hbm, u_ref, mask_hbm,
    oq_ref, ok_ref, ov_ref,
    handed, kv_send, qg_send, bias_send, kv_buf, qg_buf, bias_buf, acc,
    dz_send, dz_recv, dq_send, dq_recv, dkv_send, dkv_recv,
    q_ref, k_ref, v_ref, c_ref, mask_ref, load_sem,
    sec_sem, kv_sem, qg_sem, bias_sem, z_sem, dz_sem, dq_sem, dkv_sem,
):
    f32, bf16 = jnp.float32, jnp.bfloat16
    sec = lax.axis_index("section")
    row = lax.axis_index("ha")
    col = lax.axis_index("wa")
    own_heads = HEADS // cols_n
    tiles = 2 * cols_n
    peers = [lax.rem(col + j, cols_n) for j in range(1, cols_n)]
    has_up, has_down = row > 0, row < rows_n - 1
    inv_root = HEAD_DIM ** (-0.5)
    scale = inv_root * 1.4426950408889634

    loads = [
        pltpu.make_async_copy(src, dst, load_sem.at[n])
        for n, (src, dst) in enumerate(
            ((k_hbm, k_ref), (v_hbm, v_ref), (c_hbm, c_ref), (q_hbm, q_ref), (mask_hbm, mask_ref))
        )
    ]
    for load in loads:
        load.start()

    barrier = pltpu.get_barrier_semaphore()
    for peer in peers:
        pl.semaphore_signal(barrier, inc=1, device_id={"wa": peer}, device_id_type=MESH_ID)
    for cond, dev in (
        (has_up, {"ha": row - 1}),
        (has_down, {"ha": row + 1}),
        (sec > 0, {"section": sec - 1}),
        (sec < sections - 1, {"section": sec + 1}),
    ):
        @pl.when(cond)
        def _(dev=dev):
            pl.semaphore_signal(barrier, inc=1, device_id=dev, device_id_type=MESH_ID)

    def remote(src, dst, sems, at, dev):
        return pltpu.make_async_remote_copy(
            src_ref=src, dst_ref=dst, send_sem=sems.at[(0, *at)], recv_sem=sems.at[(1, *at)],
            device_id=dev, device_id_type=MESH_ID,
        )

    sec_copy = remote(u_ref, handed, sec_sem, (), {"section": sec - 1})

    def kv_copy(h, j):
        peer = peers[j]
        return remote(
            kv_send.at[peer * own_heads + h],
            kv_buf.at[h, 1, :, pl.ds(1 + 2 * col, 2)],
            kv_sem, (h, j), {"wa": peer},
        )

    def qg_copy(h, j):
        peer = peers[j]
        return remote(
            qg_send.at[peer * own_heads + h], qg_buf.at[h, col], qg_sem, (h, j), {"wa": peer}
        )

    def bias_copy(j):
        return remote(bias_send, bias_buf.at[col], bias_sem, (j,), {"wa": peers[j]})

    def z_copy(h, j, d):
        piece = pl.ds(1 + 2 * lax.rem(col + cols_n - j, cols_n), 2)
        return remote(
            kv_buf.at[h, 1, :, piece],
            kv_buf.at[h, 2 - 2 * d, :, piece],
            z_sem, (h, j, d), {"ha": row - 1 + 2 * d},
        )

    def z_start(h, j):
        @pl.when(has_up)
        def _():
            z_copy(h, j, 0).start()

        @pl.when(has_down)
        def _():
            z_copy(h, j, 1).start()

    def dz_copy(h, d):
        return remote(
            dz_send.at[h, d], dz_recv.at[h, d], dz_sem, (h, d), {"ha": row - 1 + 2 * d}
        )

    def dq_copy(h, j):
        peer = peers[j]
        return remote(
            dq_send.at[h, peer], dq_recv.at[col * own_heads + h], dq_sem, (h, j), {"wa": peer}
        )

    def dkv_copy(h, j):
        peer = peers[j]
        return remote(
            dkv_send.at[h, peer], dkv_recv.at[col * own_heads + h], dkv_sem, (h, j), {"wa": peer}
        )

    def head_cols(head):
        return pl.ds(pl.multiple_of(head * LANES, LANES), LANES)

    zero_tile = jnp.zeros((2, 64, LANES), bf16)
    for h in range(own_heads):
        for i in range(3):
            kv_buf[h, i, :, 0] = zero_tile
            kv_buf[h, i, :, tiles + 1] = zero_tile

    for cond, i in ((row == 0, 0), (row == rows_n - 1, 2)):
        @pl.when(cond)
        def _(i=i):
            for h in range(own_heads):
                @pl.loop(0, tiles)
                def _(t, h=h):
                    kv_buf[h, i, :, t + 1] = zero_tile

    total = (
        cols_n - 1
        + has_up.astype(jnp.int32) + has_down.astype(jnp.int32)
        + (sec > 0).astype(jnp.int32) + (sec < sections - 1).astype(jnp.int32)
    )
    pl.semaphore_wait(barrier, total)

    @pl.when(sec > 0)
    def _():
        sec_copy.start()

    def send_kv(h):
        @pl.loop(0, cols_n)
        def _(peer):
            head = peer * own_heads + h
            at = head_cols(head)
            kv_send[head, 0] = to_tiles(k_ref[:, at].astype(f32)).astype(bf16).reshape(2, 64, LANES)
            kv_send[head, 1] = to_tiles(v_ref[:, at].astype(f32)).astype(bf16).reshape(2, 64, LANES)

        for j in range(cols_n - 1):
            kv_copy(h, j).start()
        kv_buf[h, 1, :, pl.ds(1 + 2 * col, 2)] = kv_send[col * own_heads + h]
        z_start(h, 0)

    def send_qg(h):
        @pl.loop(0, cols_n)
        def _(peer):
            head = peer * own_heads + h
            at = head_cols(head)
            qg_send[head, 0] = to_tiles(q_ref[:, at].astype(f32)).astype(bf16)
            grad = c_ref[:, at].astype(f32) + handed[:, at].astype(f32)
            qg_send[head, 1] = to_tiles(grad).astype(bf16)

        for j in range(cols_n - 1):
            qg_copy(h, j).start()
        qg_buf[h, col] = qg_send[col * own_heads + h]

    loads[0].wait()
    loads[1].wait()
    send_kv(0)

    loads[4].wait()
    lane = lax.broadcasted_iota(jnp.int32, (1, LANES), 1)
    bias_send[...] = jnp.full(bias_send.shape, NEG, f32)
    for i in range(3):
        row_in = (row + (i - 1) >= 0) & (row + (i - 1) < rows_n)
        for jj in range(4):
            tile = 2 * col + (jj - 1)
            inside = row_in & (tile >= 0) & (tile < tiles)
            first = mask_ref[0, 3 * i + jj] if jj < 3 else jnp.int32(0)
            second = mask_ref[1, 3 * i + jj - 1] if jj > 0 else jnp.int32(0)
            seen = jnp.where(lane < 64, first, second) * inside.astype(jnp.int32)
            bias_send[pl.ds(4 * i + jj, 1), :] = jnp.where(seen > 0, 0.0, NEG).astype(f32)
    for j in range(cols_n - 1):
        bias_copy(j).start()
    bias_buf[col] = bias_send[...]

    @pl.when(sec == sections - 1)
    def _():
        handed[...] = jnp.zeros_like(handed)

    @pl.when(sec < sections - 1)
    def _():
        sec_copy.wait_recv()

    loads[2].wait()
    loads[3].wait()
    send_qg(0)
    for h in range(1, own_heads):
        send_kv(h)
        send_qg(h)

    def forward(h):
        for j in range(1, cols_n):
            kv_copy(h, j - 1).wait_recv()
            z_start(h, j)

    for j in range(cols_n - 1):
        bias_copy(j).wait_recv()

    nt = (((1,), (1,)), ((), ()))
    tn = (((0,), (0,)), ((), ()))

    def dot(a, b, dims):
        return lax.dot_general(a, b, dims, preferred_element_type=f32)

    def compute(h):
        acc[h] = jnp.zeros(acc.shape[1:], f32)

        @pl.loop(0, cols_n)
        def _(pair):
            query = qg_buf[h, pair, 0]
            grad = qg_buf[h, pair, 1]
            box = pl.ds(2 * pair, 4)
            key_rows = [kv_buf[h, i, 0, box].reshape(256, LANES) for i in range(3)]
            value_rows = [kv_buf[h, i, 1, box].reshape(256, LANES) for i in range(3)]
            blocks = []
            for i in range(3):
                part = dot(key_rows[i], query, nt) * scale
                for jj in range(4):
                    blocks.append(
                        part[jj * 64 : jj * 64 + 64] + bias_buf[pair, pl.ds(4 * i + jj, 1), :]
                    )
            scores = jnp.concatenate(blocks, axis=0)
            weights = jnp.exp2(scores - jnp.max(scores, axis=0, keepdims=True))
            probs = weights * (1.0 / jnp.sum(weights, axis=0, keepdims=True))
            low = probs.astype(bf16)
            grad_probs = jnp.concatenate([dot(rows, grad, nt) for rows in value_rows], axis=0)
            deltas = jnp.sum(low.astype(f32) * grad_probs, axis=0, keepdims=True)
            grad_scores = (probs * (grad_probs - deltas) * inv_root).astype(bf16)
            keys_all = jnp.concatenate(key_rows, axis=0)
            dq_send[h, pair] = dot(grad_scores, keys_all, tn).astype(bf16)
            grad_key = dot(grad_scores, query, (((1,), (0,)), ((), ())))
            grad_value = dot(low, grad, (((1,), (0,)), ((), ())))
            for i in range(3):
                at = slice(i * 256, i * 256 + 256)
                acc[h, i, 0, box] += grad_key[at].reshape(4, 64, LANES)
                acc[h, i, 1, box] += grad_value[at].reshape(4, 64, LANES)

    def finish(h):
        @pl.when(has_down)
        def _():
            dz_copy(h, 0).wait_recv()

        @pl.when(has_up)
        def _():
            dz_copy(h, 1).wait_recv()

        for cond, d in ((jnp.logical_not(has_down), 0), (jnp.logical_not(has_up), 1)):
            @pl.when(cond)
            def _(d=d):
                dz_recv[h, d] = jnp.zeros(dz_recv.shape[2:], bf16)

        @pl.loop(0, cols_n)
        def _(pair):
            for kv in range(2):
                total = (
                    acc[h, 1, kv, pl.ds(1 + 2 * pair, 2)]
                    + dz_recv[h, 0, kv, pl.ds(2 * pair, 2)].astype(f32)
                    + dz_recv[h, 1, kv, pl.ds(2 * pair, 2)].astype(f32)
                )
                dkv_send[h, pair, kv] = total.astype(bf16).reshape(128, LANES)

        for j in range(cols_n - 1):
            dkv_copy(h, j).start()
        dkv_recv[col * own_heads + h] = dkv_send[h, col]

    forward(0)
    for h in range(own_heads):
        if h + 1 < own_heads:
            forward(h + 1)
        for j in range(cols_n - 1):
            qg_copy(h, j).wait_recv()

        @pl.when(has_down)
        def _(h=h):
            for j in range(cols_n):
                z_copy(h, j, 0).wait_recv()

        @pl.when(has_up)
        def _(h=h):
            for j in range(cols_n):
                z_copy(h, j, 1).wait_recv()

        compute(h)
        for d, cond in ((0, has_up), (1, has_down)):
            @pl.when(cond)
            def _(d=d, h=h):
                for kv in range(2):
                    dz_send[h, d, kv] = acc[h, 2 * d, kv, pl.ds(1, tiles)].astype(bf16)
                dz_copy(h, d).start()
        for j in range(cols_n - 1):
            dq_copy(h, j).start()
        dq_recv[col * own_heads + h] = dq_send[h, col]
        if h > 0:
            finish(h - 1)
    finish(own_heads - 1)

    for h in range(own_heads):
        for j in range(cols_n - 1):
            dq_copy(h, j).wait_recv()

    @pl.loop(0, HEADS)
    def _(head):
        oq_ref[:, head_cols(head)] = from_tiles(dq_recv[head].astype(f32)).astype(bf16)

    for h in range(own_heads):
        for j in range(cols_n - 1):
            dkv_copy(h, j).wait_recv()

    @pl.loop(0, HEADS)
    def _(head):
        ok_ref[:, head_cols(head)] = from_tiles(dkv_recv[head, 0].astype(f32)).astype(bf16)
        ov_ref[:, head_cols(head)] = from_tiles(dkv_recv[head, 1].astype(f32)).astype(bf16)

    @pl.when(sec > 0)
    def _():
        sec_copy.wait_send()

    for j in range(cols_n - 1):
        bias_copy(j).wait_send()
        for h in range(own_heads):
            for copy in (kv_copy, qg_copy, dq_copy, dkv_copy):
                copy(h, j).wait_send()
    for d, cond in ((0, has_up), (1, has_down)):
        @pl.when(cond)
        def _(d=d):
            for h in range(own_heads):
                for j in range(cols_n):
                    z_copy(h, j, d).wait_send()
                dz_copy(h, d).wait_send()


def fused_body(queries, keys, values, cotangent, upstream, block_mask):
    sections, rows_n, cols_n = (lax.axis_size(a) for a in ("section", "ha", "wa"))
    shape = queries.shape
    tokens = shape[1] * shape[2] * shape[3]
    flat = (tokens, shape[4])
    own = HEADS // cols_n
    tiles = 2 * cols_n
    bf16, f32 = jnp.bfloat16, jnp.float32
    vmem = pl.BlockSpec(memory_space=pltpu.VMEM)
    dma = pltpu.SemaphoreType.DMA
    out = pl.pallas_call(
        functools.partial(fused_kernel, sections, rows_n, cols_n),
        out_shape=[jax.ShapeDtypeStruct(flat, bf16)] * 3,
        in_specs=[pl.BlockSpec(memory_space=pltpu.HBM)] * 6,
        out_specs=[vmem] * 3,
        scratch_shapes=[
            pltpu.VMEM(flat, bf16),
            pltpu.VMEM((HEADS, 2, 2, 64, LANES), bf16),
            pltpu.VMEM((HEADS, 2, 128, LANES), bf16),
            pltpu.VMEM((16, LANES), f32),
            pltpu.VMEM((own, 3, 2, tiles + 2, 64, LANES), bf16),
            pltpu.VMEM((own, cols_n, 2, 128, LANES), bf16),
            pltpu.VMEM((cols_n, 16, LANES), f32),
            pltpu.VMEM((own, 3, 2, tiles + 2, 64, LANES), f32),
            pltpu.VMEM((own, 2, 2, tiles, 64, LANES), bf16),
            pltpu.VMEM((own, 2, 2, tiles, 64, LANES), bf16),
            pltpu.VMEM((own, cols_n, 128, LANES), bf16),
            pltpu.VMEM((HEADS, 128, LANES), bf16),
            pltpu.VMEM((own, cols_n, 2, 128, LANES), bf16),
            pltpu.VMEM((HEADS, 2, 128, LANES), bf16),
            pltpu.VMEM(flat, bf16),
            pltpu.VMEM(flat, bf16),
            pltpu.VMEM(flat, bf16),
            pltpu.VMEM(flat, bf16),
            pltpu.SMEM((2, 9), jnp.int32),
            dma((5,)),
            dma((2,)),
            dma((2, own, cols_n - 1)),
            dma((2, own, cols_n - 1)),
            dma((2, cols_n - 1)),
            dma((2, own, cols_n, 2)),
            dma((2, own, 2)),
            dma((2, own, cols_n - 1)),
            dma((2, own, cols_n - 1)),
        ],
        compiler_params=pltpu.CompilerParams(
            collective_id=0, has_side_effects=True, vmem_limit_bytes=50 * 2**20
        ),
    )(
        queries.reshape(flat), keys.reshape(flat), values.reshape(flat),
        cotangent.reshape(flat), upstream.reshape(flat), block_mask.reshape(2, 9),
    )
    return tuple(x.reshape(shape) for x in out)


def solution(mesh):
    fits = mesh.shape["wa"] == 4
    return jax.shard_map(
        fused_body if fits else body,
        mesh=mesh,
        in_specs=(
            P("section", None, "ha", "wa", None),
            P("section", None, "ha", "wa", None),
            P("section", None, "ha", "wa", None),
            P("section", None, "ha", "wa", None),
            P("section", None, "ha", "wa", None),
            P("section", "ha", "wa", None),
        ),
        out_specs=(
            P("section", None, "ha", "wa", None),
            P("section", None, "ha", "wa", None),
            P("section", None, "ha", "wa", None),
        ),
        check_vma=False,
    )
```

```python
import functools

import jax
import jax.numpy as jnp
from jax import lax
from jax.experimental import pallas as pl
from jax.experimental.pallas import tpu as pltpu
from jax.sharding import PartitionSpec as P

HEADS = 12
HEAD_DIM = 128
TILE = 8


def passed_along(value, axis, steps):
    count = lax.axis_size(axis)
    initial, last = (max(0, -steps), min(count, count - steps))
    return lax.ppermute(value, axis, [(source, source + steps) for source in range(initial, last)])


def extended(value, sides, width):
    for axis, dim in sides:
        size, length = (lax.axis_size(axis), value.shape[dim])
        up = [(i, (i + 1) % size) for i in range(size - 1)]
        down = [(j, i) for i, j in up]
        last = lax.slice_in_dim(value, length - width, length, axis=dim)
        initial = lax.slice_in_dim(value, 0, width, axis=dim)
        before = lax.ppermute(last, axis, up)
        after = lax.ppermute(initial, axis, down)
        value = jnp.concatenate([before, value, after], axis=dim)
    return value


def window_live(mask_table, tile_row, tile_col, grid_height, grid_width):
    box_span = 3 * TILE
    offsets = jnp.arange(box_span, dtype=jnp.int32)
    rows_at = tile_row * TILE - TILE + offsets
    cols_at = tile_col * TILE - TILE + offsets
    part_of = offsets // TILE
    thirds = jnp.arange(3, dtype=jnp.int32)
    part_hot = (part_of[:, None] == thirds[None, :]).astype(jnp.float32)
    grid_mask = mask_table.reshape(3, 3).astype(jnp.float32)
    allowed = jnp.dot(jnp.dot(part_hot, grid_mask), part_hot.T)
    inside_rows = (rows_at >= 0) & (rows_at < grid_height)
    inside_cols = (cols_at >= 0) & (cols_at < grid_width)
    return (allowed > 0.5) & inside_rows[:, None] & inside_cols[None, :]


def body(queries, keys, values, cotangent, upstream, block_mask):
    handed = passed_along(upstream, "section", -1)
    paired = jnp.stack((keys, values), axis=0)
    box_kv = extended(paired, (("ha", 3), ("wa", 4)), TILE)
    grad_out = (cotangent.astype(jnp.float32) + handed.astype(jnp.float32)).astype(jnp.bfloat16)
    frames_n = queries.shape[1]
    chan_count = queries.shape[4]
    own_width = queries.shape[3]
    span_count = own_width // TILE
    box_span = 3 * TILE
    ext_width = own_width + 2 * TILE
    query_count = frames_n * TILE * own_width
    region_rows = frames_n * box_span * ext_width
    grid_height = TILE * lax.axis_size("ha")
    grid_width = own_width * lax.axis_size("wa")
    tile_row = lax.axis_index("ha")
    inv_root = HEAD_DIM ** (-0.5)
    region_live = []
    for tile_at in range(span_count):
        tile_col = lax.axis_index("wa") * span_count + tile_at
        live_cells = window_live(
            block_mask[0, 0, tile_at], tile_row, tile_col, grid_height, grid_width
        )
        placed = jnp.pad(
            live_cells, ((0, 0), (tile_at * TILE, ext_width - box_span - tile_at * TILE))
        )
        region_live.append(placed[None].reshape(region_rows))
    live_table = jnp.stack(region_live, axis=0).astype(jnp.float32)
    col_tile = jnp.arange(own_width, dtype=jnp.int32) // TILE
    query_tile = jnp.broadcast_to(col_tile[None, None, :], (frames_n, TILE, own_width)).reshape(
        query_count
    )
    tile_hot = (query_tile[:, None] == jnp.arange(span_count, dtype=jnp.int32)[None, :]).astype(
        jnp.float32
    )
    live_pairs = jnp.dot(tile_hot, live_table) > 0.5
    query_rows = queries[0].reshape(query_count, HEADS, HEAD_DIM)
    grad_rows = grad_out[0].reshape(query_count, HEADS, HEAD_DIM)
    key_rows = box_kv[0, 0].reshape(region_rows, HEADS, HEAD_DIM)
    value_rows = box_kv[1, 0].reshape(region_rows, HEADS, HEAD_DIM)
    scores = (
        jnp.einsum("qhd,khd->hqk", query_rows, key_rows, preferred_element_type=jnp.float32)
        * inv_root
    )
    scores = jnp.where(live_pairs[None], scores, -jnp.inf)
    row_max = jnp.max(scores, axis=2, keepdims=True)
    weights = jnp.exp(scores - row_max)
    softmax_probs = weights / jnp.sum(weights, axis=2, keepdims=True)
    probs_low = softmax_probs.astype(jnp.bfloat16)
    attended = jnp.einsum("hqk,khd->qhd", probs_low, value_rows, preferred_element_type=jnp.float32)
    deltas = jnp.sum(grad_rows.astype(jnp.float32) * attended, axis=2)
    grad_probs = jnp.einsum(
        "qhd,khd->hqk", grad_rows, value_rows, preferred_element_type=jnp.float32
    )
    grad_scores = (softmax_probs * (grad_probs - deltas.T[:, :, None]) * inv_root).astype(
        jnp.bfloat16
    )
    grad_query = jnp.einsum(
        "hqk,khd->qhd", grad_scores, key_rows, preferred_element_type=jnp.float32
    )
    grad_queries = grad_query.reshape(1, frames_n, TILE, own_width, chan_count).astype(jnp.bfloat16)
    weight_pair = jnp.stack((grad_scores, probs_low), axis=0)
    source_pair = jnp.stack((query_rows, grad_rows), axis=1)
    region_grads = jnp.einsum(
        "shqk,qshd->skhd", weight_pair, source_pair, preferred_element_type=jnp.float32
    )
    region_grads = region_grads.reshape(2, frames_n, box_span, ext_width, chan_count)
    col_send = jnp.concatenate(
        [region_grads[:, :, :, :TILE], region_grads[:, :, :, ext_width - TILE :]], axis=3
    ).astype(jnp.bfloat16)
    col_back = extended(col_send[None], (("wa", 4),), TILE)[0]
    back_width = col_back.shape[3]
    gap_shape = list(col_back.shape)
    gap_shape[3] = own_width - 2 * TILE
    col_gap = jnp.zeros(gap_shape, jnp.float32)
    col_folded = region_grads[:, :, :, TILE : ext_width - TILE] + jnp.concatenate(
        [
            col_back[:, :, :, :TILE].astype(jnp.float32),
            col_gap,
            col_back[:, :, :, back_width - TILE :].astype(jnp.float32),
        ],
        axis=3,
    )
    row_send = jnp.concatenate(
        [col_folded[:, :, :TILE], col_folded[:, :, 2 * TILE :]], axis=2
    ).astype(jnp.bfloat16)
    row_back = extended(row_send[None], (("ha", 3),), TILE)[0]
    folded_all = (
        col_folded[:, :, TILE : 2 * TILE]
        + row_back[:, :, :TILE].astype(jnp.float32)
        + row_back[:, :, 3 * TILE :].astype(jnp.float32)
    ).astype(jnp.bfloat16)
    grad_keys = folded_all[0][None]
    grad_values = folded_all[1][None]
    return (grad_queries, grad_keys, grad_values)


NEG = -1e30
LANES = 128
MESH_ID = pl.DeviceIdType.MESH


def to_tiles(block):
    return jnp.concatenate(
        [block[r * 16 + t * 8 : r * 16 + t * 8 + 8] for t in range(2) for r in range(8)], axis=0
    )


def from_tiles(block):
    return jnp.concatenate(
        [block[t * 64 + r * 8 : t * 64 + r * 8 + 8] for r in range(8) for t in range(2)], axis=0
    )


def fused_kernel(
    sections, rows_n, cols_n,
    q_hbm, k_hbm, v_hbm, c_hbm, u_ref, mask_hbm,
    oq_hbm, ok_hbm, ov_hbm,
    handed, kv_send, qg_send, bias_send, kv_buf, qg_buf, bias_buf, acc,
    dz_send, dz_recv, dq_send, dq_recv, dkv_send, dkv_recv,
    q_ref, k_ref, v_ref, c_ref, mask_ref, load_sem, oq_ref, ok_ref, ov_ref, store_sem,
    sec_sem, kv_sem, qg_sem, bias_sem, z_sem, dz_sem, dq_sem, dkv_sem,
):
    f32, bf16 = jnp.float32, jnp.bfloat16
    sec = lax.axis_index("section")
    row = lax.axis_index("ha")
    col = lax.axis_index("wa")
    own_heads = HEADS // cols_n
    tiles = 2 * cols_n
    peers = [lax.rem(col + j, cols_n) for j in range(1, cols_n)]
    has_up, has_down = row > 0, row < rows_n - 1
    inv_root = HEAD_DIM ** (-0.5)
    scale = inv_root * 1.4426950408889634

    loads = [
        pltpu.make_async_copy(src, dst, load_sem.at[n])
        for n, (src, dst) in enumerate(
            ((k_hbm, k_ref), (v_hbm, v_ref), (c_hbm, c_ref), (q_hbm, q_ref), (mask_hbm, mask_ref))
        )
    ]
    for load in loads:
        load.start()
    stores = [
        pltpu.make_async_copy(src, dst, store_sem.at[n])
        for n, (src, dst) in enumerate(((oq_ref, oq_hbm), (ok_ref, ok_hbm), (ov_ref, ov_hbm)))
    ]

    barrier = pltpu.get_barrier_semaphore()
    for peer in peers:
        pl.semaphore_signal(barrier, inc=1, device_id={"wa": peer}, device_id_type=MESH_ID)
    for cond, dev in (
        (has_up, {"ha": row - 1}),
        (has_down, {"ha": row + 1}),
        (sec > 0, {"section": sec - 1}),
        (sec < sections - 1, {"section": sec + 1}),
    ):
        @pl.when(cond)
        def _(dev=dev):
            pl.semaphore_signal(barrier, inc=1, device_id=dev, device_id_type=MESH_ID)

    def remote(src, dst, sems, at, dev):
        return pltpu.make_async_remote_copy(
            src_ref=src, dst_ref=dst, send_sem=sems.at[(0, *at)], recv_sem=sems.at[(1, *at)],
            device_id=dev, device_id_type=MESH_ID,
        )

    sec_copy = remote(u_ref, handed, sec_sem, (), {"section": sec - 1})

    def kv_copy(h, j):
        peer = peers[j]
        return remote(
            kv_send.at[peer * own_heads + h],
            kv_buf.at[h, 1, :, pl.ds(1 + 2 * col, 2)],
            kv_sem, (h, j), {"wa": peer},
        )

    def qg_copy(h, j):
        peer = peers[j]
        return remote(
            qg_send.at[peer * own_heads + h], qg_buf.at[h, col], qg_sem, (h, j), {"wa": peer}
        )

    def bias_copy(j):
        return remote(bias_send, bias_buf.at[col], bias_sem, (j,), {"wa": peers[j]})

    def z_copy(h, j, d):
        piece = pl.ds(1 + 2 * lax.rem(col + cols_n - j, cols_n), 2)
        return remote(
            kv_buf.at[h, 1, :, piece],
            kv_buf.at[h, 2 - 2 * d, :, piece],
            z_sem, (h, j, d), {"ha": row - 1 + 2 * d},
        )

    def z_start(h, j):
        @pl.when(has_up)
        def _():
            z_copy(h, j, 0).start()

        @pl.when(has_down)
        def _():
            z_copy(h, j, 1).start()

    def dz_copy(h, d):
        return remote(
            dz_send.at[h, d], dz_recv.at[h, d], dz_sem, (h, d), {"ha": row - 1 + 2 * d}
        )

    def dq_copy(h, j):
        peer = peers[j]
        return remote(
            dq_send.at[h, peer], dq_recv.at[col * own_heads + h], dq_sem, (h, j), {"wa": peer}
        )

    def dkv_copy(h, j):
        peer = peers[j]
        return remote(
            dkv_send.at[h, peer], dkv_recv.at[col * own_heads + h], dkv_sem, (h, j), {"wa": peer}
        )

    def head_cols(head):
        return pl.ds(pl.multiple_of(head * LANES, LANES), LANES)

    zero_tile = jnp.zeros((2, 64, LANES), bf16)
    for h in range(own_heads):
        for i in range(3):
            kv_buf[h, i, :, 0] = zero_tile
            kv_buf[h, i, :, tiles + 1] = zero_tile

    for cond, i in ((row == 0, 0), (row == rows_n - 1, 2)):
        @pl.when(cond)
        def _(i=i):
            for h in range(own_heads):
                @pl.loop(0, tiles)
                def _(t, h=h):
                    kv_buf[h, i, :, t + 1] = zero_tile

    total = (
        cols_n - 1
        + has_up.astype(jnp.int32) + has_down.astype(jnp.int32)
        + (sec > 0).astype(jnp.int32) + (sec < sections - 1).astype(jnp.int32)
    )
    pl.semaphore_wait(barrier, total)

    @pl.when(sec > 0)
    def _():
        sec_copy.start()

    def send_kv(h):
        @pl.loop(0, cols_n)
        def _(peer):
            head = peer * own_heads + h
            at = head_cols(head)
            kv_send[head, 0] = to_tiles(k_ref[:, at].astype(f32)).astype(bf16).reshape(2, 64, LANES)
            kv_send[head, 1] = to_tiles(v_ref[:, at].astype(f32)).astype(bf16).reshape(2, 64, LANES)

        for j in range(cols_n - 1):
            kv_copy(h, j).start()
        kv_buf[h, 1, :, pl.ds(1 + 2 * col, 2)] = kv_send[col * own_heads + h]
        z_start(h, 0)

    def send_qg(h):
        @pl.loop(0, cols_n)
        def _(peer):
            head = peer * own_heads + h
            at = head_cols(head)
            qg_send[head, 0] = to_tiles(q_ref[:, at].astype(f32)).astype(bf16)
            grad = c_ref[:, at].astype(f32) + handed[:, at].astype(f32)
            qg_send[head, 1] = to_tiles(grad).astype(bf16)

        for j in range(cols_n - 1):
            qg_copy(h, j).start()
        qg_buf[h, col] = qg_send[col * own_heads + h]

    loads[0].wait()
    loads[1].wait()
    send_kv(0)

    loads[4].wait()
    lane = lax.broadcasted_iota(jnp.int32, (1, LANES), 1)
    bias_send[...] = jnp.full(bias_send.shape, NEG, f32)
    for i in range(3):
        row_in = (row + (i - 1) >= 0) & (row + (i - 1) < rows_n)
        for jj in range(4):
            tile = 2 * col + (jj - 1)
            inside = row_in & (tile >= 0) & (tile < tiles)
            first = mask_ref[0, 3 * i + jj] if jj < 3 else jnp.int32(0)
            second = mask_ref[1, 3 * i + jj - 1] if jj > 0 else jnp.int32(0)
            seen = jnp.where(lane < 64, first, second) * inside.astype(jnp.int32)
            bias_send[pl.ds(4 * i + jj, 1), :] = jnp.where(seen > 0, 0.0, NEG).astype(f32)
    for j in range(cols_n - 1):
        bias_copy(j).start()
    bias_buf[col] = bias_send[...]

    @pl.when(sec == sections - 1)
    def _():
        handed[...] = jnp.zeros_like(handed)

    @pl.when(sec < sections - 1)
    def _():
        sec_copy.wait_recv()

    loads[2].wait()
    loads[3].wait()
    send_qg(0)
    for h in range(1, own_heads):
        send_kv(h)
        send_qg(h)

    def forward(h):
        for j in range(1, cols_n):
            kv_copy(h, j - 1).wait_recv()
            z_start(h, j)

    for j in range(cols_n - 1):
        bias_copy(j).wait_recv()

    nt = (((1,), (1,)), ((), ()))
    tn = (((0,), (0,)), ((), ()))

    def dot(a, b, dims):
        return lax.dot_general(a, b, dims, preferred_element_type=f32)

    def compute(h):
        acc[h] = jnp.zeros(acc.shape[1:], f32)

        @pl.loop(0, cols_n)
        def _(pair):
            query = qg_buf[h, pair, 0]
            grad = qg_buf[h, pair, 1]
            box = pl.ds(2 * pair, 4)
            key_rows = [kv_buf[h, i, 0, box].reshape(256, LANES) for i in range(3)]
            value_rows = [kv_buf[h, i, 1, box].reshape(256, LANES) for i in range(3)]
            blocks = []
            for i in range(3):
                part = dot(key_rows[i], query, nt) * scale
                for jj in range(4):
                    blocks.append(
                        part[jj * 64 : jj * 64 + 64] + bias_buf[pair, pl.ds(4 * i + jj, 1), :]
                    )
            scores = jnp.concatenate(blocks, axis=0)
            weights = jnp.exp2(scores - jnp.max(scores, axis=0, keepdims=True))
            probs = weights * (1.0 / jnp.sum(weights, axis=0, keepdims=True))
            low = probs.astype(bf16)
            grad_probs = jnp.concatenate([dot(rows, grad, nt) for rows in value_rows], axis=0)
            deltas = jnp.sum(low.astype(f32) * grad_probs, axis=0, keepdims=True)
            grad_scores = (probs * (grad_probs - deltas) * inv_root).astype(bf16)
            keys_all = jnp.concatenate(key_rows, axis=0)
            dq_send[h, pair] = dot(grad_scores, keys_all, tn).astype(bf16)
            grad_key = dot(grad_scores, query, (((1,), (0,)), ((), ())))
            grad_value = dot(low, grad, (((1,), (0,)), ((), ())))
            for i in range(3):
                at = slice(i * 256, i * 256 + 256)
                acc[h, i, 0, box] += grad_key[at].reshape(4, 64, LANES)
                acc[h, i, 1, box] += grad_value[at].reshape(4, 64, LANES)

    def finish(h):
        @pl.when(has_down)
        def _():
            dz_copy(h, 0).wait_recv()

        @pl.when(has_up)
        def _():
            dz_copy(h, 1).wait_recv()

        for cond, d in ((jnp.logical_not(has_down), 0), (jnp.logical_not(has_up), 1)):
            @pl.when(cond)
            def _(d=d):
                dz_recv[h, d] = jnp.zeros(dz_recv.shape[2:], bf16)

        @pl.loop(0, cols_n)
        def _(pair):
            for kv in range(2):
                total = (
                    acc[h, 1, kv, pl.ds(1 + 2 * pair, 2)]
                    + dz_recv[h, 0, kv, pl.ds(2 * pair, 2)].astype(f32)
                    + dz_recv[h, 1, kv, pl.ds(2 * pair, 2)].astype(f32)
                )
                dkv_send[h, pair, kv] = total.astype(bf16).reshape(128, LANES)

        for j in range(cols_n - 1):
            dkv_copy(h, j).start()
        dkv_recv[col * own_heads + h] = dkv_send[h, col]

    forward(0)
    for h in range(own_heads):
        if h + 1 < own_heads:
            forward(h + 1)
        for j in range(cols_n - 1):
            qg_copy(h, j).wait_recv()

        @pl.when(has_down)
        def _(h=h):
            for j in range(cols_n):
                z_copy(h, j, 0).wait_recv()

        @pl.when(has_up)
        def _(h=h):
            for j in range(cols_n):
                z_copy(h, j, 1).wait_recv()

        compute(h)
        for d, cond in ((0, has_up), (1, has_down)):
            @pl.when(cond)
            def _(d=d, h=h):
                for kv in range(2):
                    dz_send[h, d, kv] = acc[h, 2 * d, kv, pl.ds(1, tiles)].astype(bf16)
                dz_copy(h, d).start()
        for j in range(cols_n - 1):
            dq_copy(h, j).start()
        dq_recv[col * own_heads + h] = dq_send[h, col]
        if h > 0:
            finish(h - 1)

    for h in range(own_heads):
        for j in range(cols_n - 1):
            dq_copy(h, j).wait_recv()

    @pl.loop(0, HEADS)
    def _(head):
        oq_ref[:, head_cols(head)] = from_tiles(dq_recv[head].astype(f32)).astype(bf16)

    stores[0].start()

    def place(h):
        for j in range(cols_n - 1):
            dkv_copy(h, j).wait_recv()

        @pl.loop(0, cols_n)
        def _(peer):
            head = peer * own_heads + h
            at = head_cols(head)
            ok_ref[:, at] = from_tiles(dkv_recv[head, 0].astype(f32)).astype(bf16)
            ov_ref[:, at] = from_tiles(dkv_recv[head, 1].astype(f32)).astype(bf16)

    place(0)
    finish(own_heads - 1)
    for h in range(1, own_heads):
        place(h)
    stores[1].start()
    stores[2].start()

    @pl.when(sec > 0)
    def _():
        sec_copy.wait_send()

    for j in range(cols_n - 1):
        bias_copy(j).wait_send()
        for h in range(own_heads):
            for copy in (kv_copy, qg_copy, dq_copy, dkv_copy):
                copy(h, j).wait_send()
    for d, cond in ((0, has_up), (1, has_down)):
        @pl.when(cond)
        def _(d=d):
            for h in range(own_heads):
                for j in range(cols_n):
                    z_copy(h, j, d).wait_send()
                dz_copy(h, d).wait_send()
    for store in stores:
        store.wait()


def fused_body(queries, keys, values, cotangent, upstream, block_mask):
    sections, rows_n, cols_n = (lax.axis_size(a) for a in ("section", "ha", "wa"))
    shape = queries.shape
    tokens = shape[1] * shape[2] * shape[3]
    flat = (tokens, shape[4])
    own = HEADS // cols_n
    tiles = 2 * cols_n
    bf16, f32 = jnp.bfloat16, jnp.float32
    dma = pltpu.SemaphoreType.DMA
    out = pl.pallas_call(
        functools.partial(fused_kernel, sections, rows_n, cols_n),
        out_shape=[jax.ShapeDtypeStruct(flat, bf16)] * 3,
        in_specs=[pl.BlockSpec(memory_space=pltpu.HBM)] * 6,
        out_specs=[pl.BlockSpec(memory_space=pltpu.HBM)] * 3,
        scratch_shapes=[
            pltpu.VMEM(flat, bf16),
            pltpu.VMEM((HEADS, 2, 2, 64, LANES), bf16),
            pltpu.VMEM((HEADS, 2, 128, LANES), bf16),
            pltpu.VMEM((16, LANES), f32),
            pltpu.VMEM((own, 3, 2, tiles + 2, 64, LANES), bf16),
            pltpu.VMEM((own, cols_n, 2, 128, LANES), bf16),
            pltpu.VMEM((cols_n, 16, LANES), f32),
            pltpu.VMEM((own, 3, 2, tiles + 2, 64, LANES), f32),
            pltpu.VMEM((own, 2, 2, tiles, 64, LANES), bf16),
            pltpu.VMEM((own, 2, 2, tiles, 64, LANES), bf16),
            pltpu.VMEM((own, cols_n, 128, LANES), bf16),
            pltpu.VMEM((HEADS, 128, LANES), bf16),
            pltpu.VMEM((own, cols_n, 2, 128, LANES), bf16),
            pltpu.VMEM((HEADS, 2, 128, LANES), bf16),
            pltpu.VMEM(flat, bf16),
            pltpu.VMEM(flat, bf16),
            pltpu.VMEM(flat, bf16),
            pltpu.VMEM(flat, bf16),
            pltpu.SMEM((2, 9), jnp.int32),
            dma((5,)),
            pltpu.VMEM(flat, bf16),
            pltpu.VMEM(flat, bf16),
            pltpu.VMEM(flat, bf16),
            dma((3,)),
            dma((2,)),
            dma((2, own, cols_n - 1)),
            dma((2, own, cols_n - 1)),
            dma((2, cols_n - 1)),
            dma((2, own, cols_n, 2)),
            dma((2, own, 2)),
            dma((2, own, cols_n - 1)),
            dma((2, own, cols_n - 1)),
        ],
        compiler_params=pltpu.CompilerParams(
            collective_id=0, has_side_effects=True, vmem_limit_bytes=62 * 2**20
        ),
    )(
        queries.reshape(flat), keys.reshape(flat), values.reshape(flat),
        cotangent.reshape(flat), upstream.reshape(flat), block_mask.reshape(2, 9),
    )
    return tuple(x.reshape(shape) for x in out)


def solution(mesh):
    fits = mesh.shape["wa"] == 4
    return jax.shard_map(
        fused_body if fits else body,
        mesh=mesh,
        in_specs=(
            P("section", None, "ha", "wa", None),
            P("section", None, "ha", "wa", None),
            P("section", None, "ha", "wa", None),
            P("section", None, "ha", "wa", None),
            P("section", None, "ha", "wa", None),
            P("section", "ha", "wa", None),
        ),
        out_specs=(
            P("section", None, "ha", "wa", None),
            P("section", None, "ha", "wa", None),
            P("section", None, "ha", "wa", None),
        ),
        check_vma=False,
    )
```

```python
import functools

import jax
import jax.numpy as jnp
from jax import lax
from jax.experimental import pallas as pl
from jax.experimental.pallas import tpu as pltpu
from jax.sharding import PartitionSpec as P

HEADS = 12
HEAD_DIM = 128
TILE = 8


def passed_along(value, axis, steps):
    count = lax.axis_size(axis)
    initial, last = (max(0, -steps), min(count, count - steps))
    return lax.ppermute(value, axis, [(source, source + steps) for source in range(initial, last)])


def extended(value, sides, width):
    for axis, dim in sides:
        size, length = (lax.axis_size(axis), value.shape[dim])
        up = [(i, (i + 1) % size) for i in range(size - 1)]
        down = [(j, i) for i, j in up]
        last = lax.slice_in_dim(value, length - width, length, axis=dim)
        initial = lax.slice_in_dim(value, 0, width, axis=dim)
        before = lax.ppermute(last, axis, up)
        after = lax.ppermute(initial, axis, down)
        value = jnp.concatenate([before, value, after], axis=dim)
    return value


def window_live(mask_table, tile_row, tile_col, grid_height, grid_width):
    box_span = 3 * TILE
    offsets = jnp.arange(box_span, dtype=jnp.int32)
    rows_at = tile_row * TILE - TILE + offsets
    cols_at = tile_col * TILE - TILE + offsets
    part_of = offsets // TILE
    thirds = jnp.arange(3, dtype=jnp.int32)
    part_hot = (part_of[:, None] == thirds[None, :]).astype(jnp.float32)
    grid_mask = mask_table.reshape(3, 3).astype(jnp.float32)
    allowed = jnp.dot(jnp.dot(part_hot, grid_mask), part_hot.T)
    inside_rows = (rows_at >= 0) & (rows_at < grid_height)
    inside_cols = (cols_at >= 0) & (cols_at < grid_width)
    return (allowed > 0.5) & inside_rows[:, None] & inside_cols[None, :]


def body(queries, keys, values, cotangent, upstream, block_mask):
    handed = passed_along(upstream, "section", -1)
    paired = jnp.stack((keys, values), axis=0)
    box_kv = extended(paired, (("ha", 3), ("wa", 4)), TILE)
    grad_out = (cotangent.astype(jnp.float32) + handed.astype(jnp.float32)).astype(jnp.bfloat16)
    frames_n = queries.shape[1]
    chan_count = queries.shape[4]
    own_width = queries.shape[3]
    span_count = own_width // TILE
    box_span = 3 * TILE
    ext_width = own_width + 2 * TILE
    query_count = frames_n * TILE * own_width
    region_rows = frames_n * box_span * ext_width
    grid_height = TILE * lax.axis_size("ha")
    grid_width = own_width * lax.axis_size("wa")
    tile_row = lax.axis_index("ha")
    inv_root = HEAD_DIM ** (-0.5)
    region_live = []
    for tile_at in range(span_count):
        tile_col = lax.axis_index("wa") * span_count + tile_at
        live_cells = window_live(
            block_mask[0, 0, tile_at], tile_row, tile_col, grid_height, grid_width
        )
        placed = jnp.pad(
            live_cells, ((0, 0), (tile_at * TILE, ext_width - box_span - tile_at * TILE))
        )
        region_live.append(placed[None].reshape(region_rows))
    live_table = jnp.stack(region_live, axis=0).astype(jnp.float32)
    col_tile = jnp.arange(own_width, dtype=jnp.int32) // TILE
    query_tile = jnp.broadcast_to(col_tile[None, None, :], (frames_n, TILE, own_width)).reshape(
        query_count
    )
    tile_hot = (query_tile[:, None] == jnp.arange(span_count, dtype=jnp.int32)[None, :]).astype(
        jnp.float32
    )
    live_pairs = jnp.dot(tile_hot, live_table) > 0.5
    query_rows = queries[0].reshape(query_count, HEADS, HEAD_DIM)
    grad_rows = grad_out[0].reshape(query_count, HEADS, HEAD_DIM)
    key_rows = box_kv[0, 0].reshape(region_rows, HEADS, HEAD_DIM)
    value_rows = box_kv[1, 0].reshape(region_rows, HEADS, HEAD_DIM)
    scores = (
        jnp.einsum("qhd,khd->hqk", query_rows, key_rows, preferred_element_type=jnp.float32)
        * inv_root
    )
    scores = jnp.where(live_pairs[None], scores, -jnp.inf)
    row_max = jnp.max(scores, axis=2, keepdims=True)
    weights = jnp.exp(scores - row_max)
    softmax_probs = weights / jnp.sum(weights, axis=2, keepdims=True)
    probs_low = softmax_probs.astype(jnp.bfloat16)
    attended = jnp.einsum("hqk,khd->qhd", probs_low, value_rows, preferred_element_type=jnp.float32)
    deltas = jnp.sum(grad_rows.astype(jnp.float32) * attended, axis=2)
    grad_probs = jnp.einsum(
        "qhd,khd->hqk", grad_rows, value_rows, preferred_element_type=jnp.float32
    )
    grad_scores = (softmax_probs * (grad_probs - deltas.T[:, :, None]) * inv_root).astype(
        jnp.bfloat16
    )
    grad_query = jnp.einsum(
        "hqk,khd->qhd", grad_scores, key_rows, preferred_element_type=jnp.float32
    )
    grad_queries = grad_query.reshape(1, frames_n, TILE, own_width, chan_count).astype(jnp.bfloat16)
    weight_pair = jnp.stack((grad_scores, probs_low), axis=0)
    source_pair = jnp.stack((query_rows, grad_rows), axis=1)
    region_grads = jnp.einsum(
        "shqk,qshd->skhd", weight_pair, source_pair, preferred_element_type=jnp.float32
    )
    region_grads = region_grads.reshape(2, frames_n, box_span, ext_width, chan_count)
    col_send = jnp.concatenate(
        [region_grads[:, :, :, :TILE], region_grads[:, :, :, ext_width - TILE :]], axis=3
    ).astype(jnp.bfloat16)
    col_back = extended(col_send[None], (("wa", 4),), TILE)[0]
    back_width = col_back.shape[3]
    gap_shape = list(col_back.shape)
    gap_shape[3] = own_width - 2 * TILE
    col_gap = jnp.zeros(gap_shape, jnp.float32)
    col_folded = region_grads[:, :, :, TILE : ext_width - TILE] + jnp.concatenate(
        [
            col_back[:, :, :, :TILE].astype(jnp.float32),
            col_gap,
            col_back[:, :, :, back_width - TILE :].astype(jnp.float32),
        ],
        axis=3,
    )
    row_send = jnp.concatenate(
        [col_folded[:, :, :TILE], col_folded[:, :, 2 * TILE :]], axis=2
    ).astype(jnp.bfloat16)
    row_back = extended(row_send[None], (("ha", 3),), TILE)[0]
    folded_all = (
        col_folded[:, :, TILE : 2 * TILE]
        + row_back[:, :, :TILE].astype(jnp.float32)
        + row_back[:, :, 3 * TILE :].astype(jnp.float32)
    ).astype(jnp.bfloat16)
    grad_keys = folded_all[0][None]
    grad_values = folded_all[1][None]
    return (grad_queries, grad_keys, grad_values)


NEG = -1e30
LANES = 128
MESH_ID = pl.DeviceIdType.MESH


def to_tiles(block):
    return jnp.concatenate(
        [block[r * 16 + t * 8 : r * 16 + t * 8 + 8] for t in range(2) for r in range(8)], axis=0
    )


def from_tiles(block):
    return jnp.concatenate(
        [block[t * 64 + r * 8 : t * 64 + r * 8 + 8] for r in range(8) for t in range(2)], axis=0
    )


def fused_kernel(
    sections, rows_n, cols_n,
    q_hbm, k_hbm, v_hbm, c_hbm, u_ref, mask_hbm,
    oq_hbm, ok_hbm, ov_hbm,
    handed, kv_send, qg_send, bias_send, kv_buf, qg_buf, bias_buf, acc,
    dz_send, dz_recv, dq_send, dq_recv, dkv_send, dkv_recv,
    q_ref, k_ref, v_ref, c_ref, mask_ref, load_sem, oq_ref, ok_ref, ov_ref, store_sem,
    sec_sem, kv_sem, qg_sem, bias_sem, z_sem, dz_sem, dq_sem, dkv_sem,
):
    f32, bf16 = jnp.float32, jnp.bfloat16
    sec = lax.axis_index("section")
    row = lax.axis_index("ha")
    col = lax.axis_index("wa")
    own_heads = HEADS // cols_n
    tiles = 2 * cols_n
    peers = [lax.rem(col + j, cols_n) for j in range(1, cols_n)]
    has_up, has_down = row > 0, row < rows_n - 1
    inv_root = HEAD_DIM ** (-0.5)
    scale = inv_root * 1.4426950408889634

    loads = [
        pltpu.make_async_copy(src, dst, load_sem.at[n])
        for n, (src, dst) in enumerate(
            ((k_hbm, k_ref), (v_hbm, v_ref), (c_hbm, c_ref), (q_hbm, q_ref), (mask_hbm, mask_ref))
        )
    ]
    for load in loads:
        load.start()
    stores = [
        pltpu.make_async_copy(src, dst, store_sem.at[n])
        for n, (src, dst) in enumerate(((oq_ref, oq_hbm), (ok_ref, ok_hbm), (ov_ref, ov_hbm)))
    ]

    barrier = pltpu.get_barrier_semaphore()
    for peer in peers:
        pl.semaphore_signal(barrier, inc=1, device_id={"wa": peer}, device_id_type=MESH_ID)
    for cond, dev in (
        (has_up, {"ha": row - 1}),
        (has_down, {"ha": row + 1}),
        (sec > 0, {"section": sec - 1}),
        (sec < sections - 1, {"section": sec + 1}),
    ):
        @pl.when(cond)
        def _(dev=dev):
            pl.semaphore_signal(barrier, inc=1, device_id=dev, device_id_type=MESH_ID)

    def remote(src, dst, sems, at, dev):
        return pltpu.make_async_remote_copy(
            src_ref=src, dst_ref=dst, send_sem=sems.at[(0, *at)], recv_sem=sems.at[(1, *at)],
            device_id=dev, device_id_type=MESH_ID,
        )

    sec_copy = remote(u_ref, handed, sec_sem, (), {"section": sec - 1})

    def kv_copy(h, j):
        peer = peers[j]
        return remote(
            kv_send.at[peer * own_heads + h],
            kv_buf.at[h, 1, :, pl.ds(1 + 2 * col, 2)],
            kv_sem, (h, j), {"wa": peer},
        )

    def qg_copy(h, j):
        peer = peers[j]
        return remote(
            qg_send.at[peer * own_heads + h], qg_buf.at[h, col], qg_sem, (h, j), {"wa": peer}
        )

    def bias_copy(j):
        return remote(bias_send, bias_buf.at[col], bias_sem, (j,), {"wa": peers[j]})

    def z_copy(h, j, d):
        piece = pl.ds(1 + 2 * lax.rem(col + cols_n - j, cols_n), 2)
        return remote(
            kv_buf.at[h, 1, :, piece],
            kv_buf.at[h, 2 - 2 * d, :, piece],
            z_sem, (h, j, d), {"ha": row - 1 + 2 * d},
        )

    def z_start(h, j):
        @pl.when(has_up)
        def _():
            z_copy(h, j, 0).start()

        @pl.when(has_down)
        def _():
            z_copy(h, j, 1).start()

    def dz_copy(h, pair, d):
        piece = pl.ds(2 * pair, 2)
        return remote(
            dz_send.at[h, d, :, piece], dz_recv.at[h, d, :, piece],
            dz_sem, (h, pair, d), {"ha": row - 1 + 2 * d},
        )

    def dz_start(h, pair):
        for d, cond in ((0, has_up), (1, has_down)):
            @pl.when(cond)
            def _(d=d):
                for kv in range(2):
                    dz_send[h, d, kv, pl.ds(2 * pair, 2)] = acc[
                        h, 2 * d, kv, pl.ds(1 + 2 * pair, 2)
                    ].astype(bf16)
                dz_copy(h, pair, d).start()

    def dq_copy(h, j):
        peer = peers[j]
        return remote(
            dq_send.at[h, peer], dq_recv.at[col * own_heads + h], dq_sem, (h, j), {"wa": peer}
        )

    def dkv_copy(h, j):
        peer = lax.rem(col + j + 1, cols_n)
        return remote(
            dkv_send.at[h, peer], dkv_recv.at[col * own_heads + h], dkv_sem, (h, j), {"wa": peer}
        )

    def head_cols(head):
        return pl.ds(pl.multiple_of(head * LANES, LANES), LANES)

    zero_tile = jnp.zeros((2, 64, LANES), bf16)
    for h in range(own_heads):
        for i in range(3):
            kv_buf[h, i, :, 0] = zero_tile
            kv_buf[h, i, :, tiles + 1] = zero_tile

    for cond, i in ((row == 0, 0), (row == rows_n - 1, 2)):
        @pl.when(cond)
        def _(i=i):
            for h in range(own_heads):
                @pl.loop(0, tiles)
                def _(t, h=h):
                    kv_buf[h, i, :, t + 1] = zero_tile

    for d, cond in ((0, row == rows_n - 1), (1, row == 0)):
        @pl.when(cond)
        def _(d=d):
            for h in range(own_heads):
                dz_recv[h, d] = jnp.zeros(dz_recv.shape[2:], bf16)

    total = (
        cols_n - 1
        + has_up.astype(jnp.int32) + has_down.astype(jnp.int32)
        + (sec > 0).astype(jnp.int32) + (sec < sections - 1).astype(jnp.int32)
    )
    pl.semaphore_wait(barrier, total)

    @pl.when(sec > 0)
    def _():
        sec_copy.start()

    def send_kv(h):
        @pl.loop(0, cols_n)
        def _(peer):
            head = peer * own_heads + h
            at = head_cols(head)
            kv_send[head, 0] = to_tiles(k_ref[:, at].astype(f32)).astype(bf16).reshape(2, 64, LANES)
            kv_send[head, 1] = to_tiles(v_ref[:, at].astype(f32)).astype(bf16).reshape(2, 64, LANES)

        for j in range(cols_n - 1):
            kv_copy(h, j).start()
        kv_buf[h, 1, :, pl.ds(1 + 2 * col, 2)] = kv_send[col * own_heads + h]
        z_start(h, 0)

    def send_qg(h):
        @pl.loop(0, cols_n)
        def _(peer):
            head = peer * own_heads + h
            at = head_cols(head)
            qg_send[head, 0] = to_tiles(q_ref[:, at].astype(f32)).astype(bf16)
            grad = c_ref[:, at].astype(f32) + handed[:, at].astype(f32)
            qg_send[head, 1] = to_tiles(grad).astype(bf16)

        for j in range(cols_n - 1):
            qg_copy(h, j).start()
        qg_buf[h, col] = qg_send[col * own_heads + h]

    loads[0].wait()
    loads[1].wait()
    send_kv(0)

    loads[4].wait()
    lane = lax.broadcasted_iota(jnp.int32, (1, LANES), 1)
    bias_send[...] = jnp.full(bias_send.shape, NEG, f32)
    for i in range(3):
        row_in = (row + (i - 1) >= 0) & (row + (i - 1) < rows_n)
        for jj in range(4):
            tile = 2 * col + (jj - 1)
            inside = row_in & (tile >= 0) & (tile < tiles)
            first = mask_ref[0, 3 * i + jj] if jj < 3 else jnp.int32(0)
            second = mask_ref[1, 3 * i + jj - 1] if jj > 0 else jnp.int32(0)
            seen = jnp.where(lane < 64, first, second) * inside.astype(jnp.int32)
            bias_send[pl.ds(4 * i + jj, 1), :] = jnp.where(seen > 0, 0.0, NEG).astype(f32)
    for j in range(cols_n - 1):
        bias_copy(j).start()
    bias_buf[col] = bias_send[...]

    @pl.when(sec == sections - 1)
    def _():
        handed[...] = jnp.zeros_like(handed)

    @pl.when(sec < sections - 1)
    def _():
        sec_copy.wait_recv()

    loads[2].wait()
    loads[3].wait()
    send_qg(0)
    for h in range(1, own_heads):
        send_kv(h)
        send_qg(h)

    def forward(h):
        for j in range(1, cols_n):
            kv_copy(h, j - 1).wait_recv()
            z_start(h, j)

    for j in range(cols_n - 1):
        bias_copy(j).wait_recv()

    nt = (((1,), (1,)), ((), ()))
    tn = (((0,), (0,)), ((), ()))

    def dot(a, b, dims):
        return lax.dot_general(a, b, dims, preferred_element_type=f32)

    def compute(h):
        acc[h] = jnp.zeros(acc.shape[1:], f32)

        @pl.loop(0, cols_n)
        def _(pair):
            query = qg_buf[h, pair, 0]
            grad = qg_buf[h, pair, 1]
            box = pl.ds(2 * pair, 4)
            key_rows = [kv_buf[h, i, 0, box].reshape(256, LANES) for i in range(3)]
            value_rows = [kv_buf[h, i, 1, box].reshape(256, LANES) for i in range(3)]
            blocks = []
            for i in range(3):
                part = dot(key_rows[i], query, nt) * scale
                for jj in range(4):
                    blocks.append(
                        part[jj * 64 : jj * 64 + 64] + bias_buf[pair, pl.ds(4 * i + jj, 1), :]
                    )
            scores = jnp.concatenate(blocks, axis=0)
            weights = jnp.exp2(scores - jnp.max(scores, axis=0, keepdims=True))
            probs = weights * (1.0 / jnp.sum(weights, axis=0, keepdims=True))
            low = probs.astype(bf16)
            grad_probs = jnp.concatenate([dot(rows, grad, nt) for rows in value_rows], axis=0)
            deltas = jnp.sum(low.astype(f32) * grad_probs, axis=0, keepdims=True)
            grad_scores = (probs * (grad_probs - deltas) * inv_root).astype(bf16)
            keys_all = jnp.concatenate(key_rows, axis=0)
            dq_send[h, pair] = dot(grad_scores, keys_all, tn).astype(bf16)
            grad_key = dot(grad_scores, query, (((1,), (0,)), ((), ())))
            grad_value = dot(low, grad, (((1,), (0,)), ((), ())))
            for i in range(3):
                at = slice(i * 256, i * 256 + 256)
                acc[h, i, 0, box] += grad_key[at].reshape(4, 64, LANES)
                acc[h, i, 1, box] += grad_value[at].reshape(4, 64, LANES)

            @pl.when(pair > 0)
            def _():
                dz_start(h, pair - 1)

        dz_start(h, cols_n - 1)

    def finish(h):
        @pl.loop(0, cols_n)
        def _(pair):
            @pl.when(has_down)
            def _():
                dz_copy(h, pair, 0).wait_recv()

            @pl.when(has_up)
            def _():
                dz_copy(h, pair, 1).wait_recv()

            for kv in range(2):
                total = (
                    acc[h, 1, kv, pl.ds(1 + 2 * pair, 2)]
                    + dz_recv[h, 0, kv, pl.ds(2 * pair, 2)].astype(f32)
                    + dz_recv[h, 1, kv, pl.ds(2 * pair, 2)].astype(f32)
                )
                dkv_send[h, pair, kv] = total.astype(bf16).reshape(128, LANES)

            @pl.when(pair != col)
            def _():
                dkv_copy(h, lax.rem(pair - col + cols_n - 1, cols_n)).start()

        dkv_recv[col * own_heads + h] = dkv_send[h, col]

    forward(0)
    for h in range(own_heads):
        if h + 1 < own_heads:
            forward(h + 1)
        for j in range(cols_n - 1):
            qg_copy(h, j).wait_recv()

        @pl.when(has_down)
        def _(h=h):
            for j in range(cols_n):
                z_copy(h, j, 0).wait_recv()

        @pl.when(has_up)
        def _(h=h):
            for j in range(cols_n):
                z_copy(h, j, 1).wait_recv()

        compute(h)
        for j in range(cols_n - 1):
            dq_copy(h, j).start()
        dq_recv[col * own_heads + h] = dq_send[h, col]
        if h > 0:
            finish(h - 1)

    for h in range(own_heads):
        for j in range(cols_n - 1):
            dq_copy(h, j).wait_recv()

    @pl.loop(0, HEADS)
    def _(head):
        oq_ref[:, head_cols(head)] = from_tiles(dq_recv[head].astype(f32)).astype(bf16)

    stores[0].start()

    def place(h):
        for j in range(cols_n - 1):
            dkv_copy(h, j).wait_recv()

        @pl.loop(0, cols_n)
        def _(peer):
            head = peer * own_heads + h
            at = head_cols(head)
            ok_ref[:, at] = from_tiles(dkv_recv[head, 0].astype(f32)).astype(bf16)
            ov_ref[:, at] = from_tiles(dkv_recv[head, 1].astype(f32)).astype(bf16)

    place(0)
    finish(own_heads - 1)
    for h in range(1, own_heads):
        place(h)
    stores[1].start()
    stores[2].start()

    @pl.when(sec > 0)
    def _():
        sec_copy.wait_send()

    for j in range(cols_n - 1):
        bias_copy(j).wait_send()
        for h in range(own_heads):
            for copy in (kv_copy, qg_copy, dq_copy, dkv_copy):
                copy(h, j).wait_send()
    for d, cond in ((0, has_up), (1, has_down)):
        @pl.when(cond)
        def _(d=d):
            for h in range(own_heads):
                for j in range(cols_n):
                    z_copy(h, j, d).wait_send()
                    dz_copy(h, j, d).wait_send()
    for store in stores:
        store.wait()


def fused_body(queries, keys, values, cotangent, upstream, block_mask):
    sections, rows_n, cols_n = (lax.axis_size(a) for a in ("section", "ha", "wa"))
    shape = queries.shape
    tokens = shape[1] * shape[2] * shape[3]
    flat = (tokens, shape[4])
    own = HEADS // cols_n
    tiles = 2 * cols_n
    bf16, f32 = jnp.bfloat16, jnp.float32
    dma = pltpu.SemaphoreType.DMA
    out = pl.pallas_call(
        functools.partial(fused_kernel, sections, rows_n, cols_n),
        out_shape=[jax.ShapeDtypeStruct(flat, bf16)] * 3,
        in_specs=[pl.BlockSpec(memory_space=pltpu.HBM)] * 6,
        out_specs=[pl.BlockSpec(memory_space=pltpu.HBM)] * 3,
        scratch_shapes=[
            pltpu.VMEM(flat, bf16),
            pltpu.VMEM((HEADS, 2, 2, 64, LANES), bf16),
            pltpu.VMEM((HEADS, 2, 128, LANES), bf16),
            pltpu.VMEM((16, LANES), f32),
            pltpu.VMEM((own, 3, 2, tiles + 2, 64, LANES), bf16),
            pltpu.VMEM((own, cols_n, 2, 128, LANES), bf16),
            pltpu.VMEM((cols_n, 16, LANES), f32),
            pltpu.VMEM((own, 3, 2, tiles + 2, 64, LANES), f32),
            pltpu.VMEM((own, 2, 2, tiles, 64, LANES), bf16),
            pltpu.VMEM((own, 2, 2, tiles, 64, LANES), bf16),
            pltpu.VMEM((own, cols_n, 128, LANES), bf16),
            pltpu.VMEM((HEADS, 128, LANES), bf16),
            pltpu.VMEM((own, cols_n, 2, 128, LANES), bf16),
            pltpu.VMEM((HEADS, 2, 128, LANES), bf16),
            pltpu.VMEM(flat, bf16),
            pltpu.VMEM(flat, bf16),
            pltpu.VMEM(flat, bf16),
            pltpu.VMEM(flat, bf16),
            pltpu.SMEM((2, 9), jnp.int32),
            dma((5,)),
            pltpu.VMEM(flat, bf16),
            pltpu.VMEM(flat, bf16),
            pltpu.VMEM(flat, bf16),
            dma((3,)),
            dma((2,)),
            dma((2, own, cols_n - 1)),
            dma((2, own, cols_n - 1)),
            dma((2, cols_n - 1)),
            dma((2, own, cols_n, 2)),
            dma((2, own, cols_n, 2)),
            dma((2, own, cols_n - 1)),
            dma((2, own, cols_n - 1)),
        ],
        compiler_params=pltpu.CompilerParams(
            collective_id=0, has_side_effects=True, vmem_limit_bytes=62 * 2**20
        ),
    )(
        queries.reshape(flat), keys.reshape(flat), values.reshape(flat),
        cotangent.reshape(flat), upstream.reshape(flat), block_mask.reshape(2, 9),
    )
    return tuple(x.reshape(shape) for x in out)


def solution(mesh):
    fits = mesh.shape["wa"] == 4
    return jax.shard_map(
        fused_body if fits else body,
        mesh=mesh,
        in_specs=(
            P("section", None, "ha", "wa", None),
            P("section", None, "ha", "wa", None),
            P("section", None, "ha", "wa", None),
            P("section", None, "ha", "wa", None),
            P("section", None, "ha", "wa", None),
            P("section", "ha", "wa", None),
        ),
        out_specs=(
            P("section", None, "ha", "wa", None),
            P("section", None, "ha", "wa", None),
            P("section", None, "ha", "wa", None),
        ),
        check_vma=False,
    )
```

```python
import functools

import jax
import jax.numpy as jnp
from jax import lax
from jax.experimental import pallas as pl
from jax.experimental.pallas import tpu as pltpu
from jax.sharding import PartitionSpec as P

HEADS = 12
HEAD_DIM = 128
TILE = 8


def passed_along(value, axis, steps):
    count = lax.axis_size(axis)
    initial, last = (max(0, -steps), min(count, count - steps))
    return lax.ppermute(value, axis, [(source, source + steps) for source in range(initial, last)])


def extended(value, sides, width):
    for axis, dim in sides:
        size, length = (lax.axis_size(axis), value.shape[dim])
        up = [(i, (i + 1) % size) for i in range(size - 1)]
        down = [(j, i) for i, j in up]
        last = lax.slice_in_dim(value, length - width, length, axis=dim)
        initial = lax.slice_in_dim(value, 0, width, axis=dim)
        before = lax.ppermute(last, axis, up)
        after = lax.ppermute(initial, axis, down)
        value = jnp.concatenate([before, value, after], axis=dim)
    return value


def window_live(mask_table, tile_row, tile_col, grid_height, grid_width):
    box_span = 3 * TILE
    offsets = jnp.arange(box_span, dtype=jnp.int32)
    rows_at = tile_row * TILE - TILE + offsets
    cols_at = tile_col * TILE - TILE + offsets
    part_of = offsets // TILE
    thirds = jnp.arange(3, dtype=jnp.int32)
    part_hot = (part_of[:, None] == thirds[None, :]).astype(jnp.float32)
    grid_mask = mask_table.reshape(3, 3).astype(jnp.float32)
    allowed = jnp.dot(jnp.dot(part_hot, grid_mask), part_hot.T)
    inside_rows = (rows_at >= 0) & (rows_at < grid_height)
    inside_cols = (cols_at >= 0) & (cols_at < grid_width)
    return (allowed > 0.5) & inside_rows[:, None] & inside_cols[None, :]


def body(queries, keys, values, cotangent, upstream, block_mask):
    handed = passed_along(upstream, "section", -1)
    paired = jnp.stack((keys, values), axis=0)
    box_kv = extended(paired, (("ha", 3), ("wa", 4)), TILE)
    grad_out = (cotangent.astype(jnp.float32) + handed.astype(jnp.float32)).astype(jnp.bfloat16)
    frames_n = queries.shape[1]
    chan_count = queries.shape[4]
    own_width = queries.shape[3]
    span_count = own_width // TILE
    box_span = 3 * TILE
    ext_width = own_width + 2 * TILE
    query_count = frames_n * TILE * own_width
    region_rows = frames_n * box_span * ext_width
    grid_height = TILE * lax.axis_size("ha")
    grid_width = own_width * lax.axis_size("wa")
    tile_row = lax.axis_index("ha")
    inv_root = HEAD_DIM ** (-0.5)
    region_live = []
    for tile_at in range(span_count):
        tile_col = lax.axis_index("wa") * span_count + tile_at
        live_cells = window_live(
            block_mask[0, 0, tile_at], tile_row, tile_col, grid_height, grid_width
        )
        placed = jnp.pad(
            live_cells, ((0, 0), (tile_at * TILE, ext_width - box_span - tile_at * TILE))
        )
        region_live.append(placed[None].reshape(region_rows))
    live_table = jnp.stack(region_live, axis=0).astype(jnp.float32)
    col_tile = jnp.arange(own_width, dtype=jnp.int32) // TILE
    query_tile = jnp.broadcast_to(col_tile[None, None, :], (frames_n, TILE, own_width)).reshape(
        query_count
    )
    tile_hot = (query_tile[:, None] == jnp.arange(span_count, dtype=jnp.int32)[None, :]).astype(
        jnp.float32
    )
    live_pairs = jnp.dot(tile_hot, live_table) > 0.5
    query_rows = queries[0].reshape(query_count, HEADS, HEAD_DIM)
    grad_rows = grad_out[0].reshape(query_count, HEADS, HEAD_DIM)
    key_rows = box_kv[0, 0].reshape(region_rows, HEADS, HEAD_DIM)
    value_rows = box_kv[1, 0].reshape(region_rows, HEADS, HEAD_DIM)
    scores = (
        jnp.einsum("qhd,khd->hqk", query_rows, key_rows, preferred_element_type=jnp.float32)
        * inv_root
    )
    scores = jnp.where(live_pairs[None], scores, -jnp.inf)
    row_max = jnp.max(scores, axis=2, keepdims=True)
    weights = jnp.exp(scores - row_max)
    softmax_probs = weights / jnp.sum(weights, axis=2, keepdims=True)
    probs_low = softmax_probs.astype(jnp.bfloat16)
    attended = jnp.einsum("hqk,khd->qhd", probs_low, value_rows, preferred_element_type=jnp.float32)
    deltas = jnp.sum(grad_rows.astype(jnp.float32) * attended, axis=2)
    grad_probs = jnp.einsum(
        "qhd,khd->hqk", grad_rows, value_rows, preferred_element_type=jnp.float32
    )
    grad_scores = (softmax_probs * (grad_probs - deltas.T[:, :, None]) * inv_root).astype(
        jnp.bfloat16
    )
    grad_query = jnp.einsum(
        "hqk,khd->qhd", grad_scores, key_rows, preferred_element_type=jnp.float32
    )
    grad_queries = grad_query.reshape(1, frames_n, TILE, own_width, chan_count).astype(jnp.bfloat16)
    weight_pair = jnp.stack((grad_scores, probs_low), axis=0)
    source_pair = jnp.stack((query_rows, grad_rows), axis=1)
    region_grads = jnp.einsum(
        "shqk,qshd->skhd", weight_pair, source_pair, preferred_element_type=jnp.float32
    )
    region_grads = region_grads.reshape(2, frames_n, box_span, ext_width, chan_count)
    col_send = jnp.concatenate(
        [region_grads[:, :, :, :TILE], region_grads[:, :, :, ext_width - TILE :]], axis=3
    ).astype(jnp.bfloat16)
    col_back = extended(col_send[None], (("wa", 4),), TILE)[0]
    back_width = col_back.shape[3]
    gap_shape = list(col_back.shape)
    gap_shape[3] = own_width - 2 * TILE
    col_gap = jnp.zeros(gap_shape, jnp.float32)
    col_folded = region_grads[:, :, :, TILE : ext_width - TILE] + jnp.concatenate(
        [
            col_back[:, :, :, :TILE].astype(jnp.float32),
            col_gap,
            col_back[:, :, :, back_width - TILE :].astype(jnp.float32),
        ],
        axis=3,
    )
    row_send = jnp.concatenate(
        [col_folded[:, :, :TILE], col_folded[:, :, 2 * TILE :]], axis=2
    ).astype(jnp.bfloat16)
    row_back = extended(row_send[None], (("ha", 3),), TILE)[0]
    folded_all = (
        col_folded[:, :, TILE : 2 * TILE]
        + row_back[:, :, :TILE].astype(jnp.float32)
        + row_back[:, :, 3 * TILE :].astype(jnp.float32)
    ).astype(jnp.bfloat16)
    grad_keys = folded_all[0][None]
    grad_values = folded_all[1][None]
    return (grad_queries, grad_keys, grad_values)


NEG = -1e30
LANES = 128
MESH_ID = pl.DeviceIdType.MESH


def to_tiles(block):
    return jnp.concatenate(
        [block[r * 16 + t * 8 : r * 16 + t * 8 + 8] for t in range(2) for r in range(8)], axis=0
    )


def from_tiles(block):
    return jnp.concatenate(
        [block[t * 64 + r * 8 : t * 64 + r * 8 + 8] for r in range(8) for t in range(2)], axis=0
    )


def fused_kernel(
    sections, rows_n, cols_n,
    q_hbm, k_hbm, v_hbm, c_hbm, u_ref, mask_hbm,
    oq_hbm, ok_hbm, ov_hbm,
    handed, kv_send, qg_send, bias_send, kv_buf, qg_buf, bias_buf, acc,
    dz_send, dz_recv, dq_send, dq_recv, dkv_send, dkv_recv,
    q_ref, k_ref, v_ref, c_ref, mask_ref, load_sem, oq_ref, ok_ref, ov_ref, store_sem,
    sec_sem, kv_sem, qg_sem, bias_sem, z_sem, dz_sem, dq_sem, dkv_sem,
):
    f32, bf16 = jnp.float32, jnp.bfloat16
    sec = lax.axis_index("section")
    row = lax.axis_index("ha")
    col = lax.axis_index("wa")
    own_heads = HEADS // cols_n
    tiles = 2 * cols_n
    peers = [lax.rem(col + j, cols_n) for j in range(1, cols_n)]
    has_up, has_down = row > 0, row < rows_n - 1
    inv_root = HEAD_DIM ** (-0.5)
    scale = inv_root * 1.4426950408889634

    loads = [
        pltpu.make_async_copy(src, dst, load_sem.at[n])
        for n, (src, dst) in enumerate(
            ((k_hbm, k_ref), (v_hbm, v_ref), (c_hbm, c_ref), (q_hbm, q_ref), (mask_hbm, mask_ref))
        )
    ]
    for load in loads:
        load.start()
    stores = [
        pltpu.make_async_copy(src, dst, store_sem.at[n])
        for n, (src, dst) in enumerate(((oq_ref, oq_hbm), (ok_ref, ok_hbm), (ov_ref, ov_hbm)))
    ]

    barrier = pltpu.get_barrier_semaphore()
    for peer in peers:
        pl.semaphore_signal(barrier, inc=1, device_id={"wa": peer}, device_id_type=MESH_ID)
    for cond, dev in (
        (has_up, {"ha": row - 1}),
        (has_down, {"ha": row + 1}),
        (sec > 0, {"section": sec - 1}),
        (sec < sections - 1, {"section": sec + 1}),
    ):
        @pl.when(cond)
        def _(dev=dev):
            pl.semaphore_signal(barrier, inc=1, device_id=dev, device_id_type=MESH_ID)

    def remote(src, dst, sems, at, dev):
        return pltpu.make_async_remote_copy(
            src_ref=src, dst_ref=dst, send_sem=sems.at[(0, *at)], recv_sem=sems.at[(1, *at)],
            device_id=dev, device_id_type=MESH_ID,
        )

    sec_copy = remote(u_ref, handed, sec_sem, (), {"section": sec - 1})

    def kv_copy(h, j):
        peer = peers[j]
        return remote(
            kv_send.at[peer * own_heads + h],
            kv_buf.at[h, 1, :, pl.ds(1 + 2 * col, 2)],
            kv_sem, (h, j), {"wa": peer},
        )

    def qg_copy(h, j):
        peer = peers[j]
        return remote(
            qg_send.at[peer * own_heads + h], qg_buf.at[h, col], qg_sem, (h, j), {"wa": peer}
        )

    def bias_copy(j):
        return remote(bias_send, bias_buf.at[col], bias_sem, (j,), {"wa": peers[j]})

    def z_copy(h, j, d):
        piece = pl.ds(1 + 2 * lax.rem(col + cols_n - j, cols_n), 2)
        return remote(
            kv_buf.at[h, 1, :, piece],
            kv_buf.at[h, 2 - 2 * d, :, piece],
            z_sem, (h, j, d), {"ha": row - 1 + 2 * d},
        )

    def z_start(h, j):
        @pl.when(has_up)
        def _():
            z_copy(h, j, 0).start()

        @pl.when(has_down)
        def _():
            z_copy(h, j, 1).start()

    def dz_copy(h, pair, d):
        piece = pl.ds(2 * pair, 2)
        return remote(
            dz_send.at[h, d, :, piece], dz_recv.at[h, d, :, piece],
            dz_sem, (h, pair, d), {"ha": row - 1 + 2 * d},
        )

    def dz_start(h, pair):
        for d, cond in ((0, has_up), (1, has_down)):
            @pl.when(cond)
            def _(d=d):
                for kv in range(2):
                    dz_send[h, d, kv, pl.ds(2 * pair, 2)] = acc[
                        h, 2 * d, kv, pl.ds(1 + 2 * pair, 2)
                    ].astype(bf16)
                dz_copy(h, pair, d).start()

    def dq_copy(h, j):
        peer = peers[j]
        return remote(
            dq_send.at[h, peer], dq_recv.at[col * own_heads + h], dq_sem, (h, j), {"wa": peer}
        )

    def dkv_copy(h, j):
        peer = lax.rem(col + j + 1, cols_n)
        return remote(
            dkv_send.at[h, peer], dkv_recv.at[col * own_heads + h], dkv_sem, (h, j), {"wa": peer}
        )

    def head_cols(head):
        return pl.ds(pl.multiple_of(head * LANES, LANES), LANES)

    zero_tile = jnp.zeros((2, 64, LANES), bf16)
    for h in range(own_heads):
        for i in range(3):
            kv_buf[h, i, :, 0] = zero_tile
            kv_buf[h, i, :, tiles + 1] = zero_tile

    for cond, i in ((row == 0, 0), (row == rows_n - 1, 2)):
        @pl.when(cond)
        def _(i=i):
            for h in range(own_heads):
                @pl.loop(0, tiles)
                def _(t, h=h):
                    kv_buf[h, i, :, t + 1] = zero_tile

    for d, cond in ((0, row == rows_n - 1), (1, row == 0)):
        @pl.when(cond)
        def _(d=d):
            for h in range(own_heads):
                dz_recv[h, d] = jnp.zeros(dz_recv.shape[2:], bf16)

    for h in range(own_heads):
        acc[h] = jnp.zeros(acc.shape[1:], f32)

    total = (
        cols_n - 1
        + has_up.astype(jnp.int32) + has_down.astype(jnp.int32)
        + (sec > 0).astype(jnp.int32) + (sec < sections - 1).astype(jnp.int32)
    )
    pl.semaphore_wait(barrier, total)

    @pl.when(sec > 0)
    def _():
        sec_copy.start()

    def send_kv(h):
        @pl.loop(0, cols_n)
        def _(peer):
            head = peer * own_heads + h
            at = head_cols(head)
            kv_send[head, 0] = to_tiles(k_ref[:, at].astype(f32)).astype(bf16).reshape(2, 64, LANES)
            kv_send[head, 1] = to_tiles(v_ref[:, at].astype(f32)).astype(bf16).reshape(2, 64, LANES)

        for j in range(cols_n - 1):
            kv_copy(h, j).start()
        kv_buf[h, 1, :, pl.ds(1 + 2 * col, 2)] = kv_send[col * own_heads + h]
        z_start(h, 0)

    def send_qg(h):
        @pl.loop(0, cols_n)
        def _(peer):
            head = peer * own_heads + h
            at = head_cols(head)
            qg_send[head, 0] = to_tiles(q_ref[:, at].astype(f32)).astype(bf16)
            grad = c_ref[:, at].astype(f32) + handed[:, at].astype(f32)
            qg_send[head, 1] = to_tiles(grad).astype(bf16)

        for j in range(cols_n - 1):
            qg_copy(h, j).start()
        qg_buf[h, col] = qg_send[col * own_heads + h]

    loads[0].wait()
    loads[1].wait()
    send_kv(0)

    loads[4].wait()
    lane = lax.broadcasted_iota(jnp.int32, (1, LANES), 1)
    bias_send[...] = jnp.full(bias_send.shape, NEG, f32)
    for i in range(3):
        row_in = (row + (i - 1) >= 0) & (row + (i - 1) < rows_n)
        for jj in range(4):
            tile = 2 * col + (jj - 1)
            inside = row_in & (tile >= 0) & (tile < tiles)
            first = mask_ref[0, 3 * i + jj] if jj < 3 else jnp.int32(0)
            second = mask_ref[1, 3 * i + jj - 1] if jj > 0 else jnp.int32(0)
            seen = jnp.where(lane < 64, first, second) * inside.astype(jnp.int32)
            bias_send[pl.ds(4 * i + jj, 1), :] = jnp.where(seen > 0, 0.0, NEG).astype(f32)
    for j in range(cols_n - 1):
        bias_copy(j).start()
    bias_buf[col] = bias_send[...]

    @pl.when(sec == sections - 1)
    def _():
        handed[...] = jnp.zeros_like(handed)

    @pl.when(sec < sections - 1)
    def _():
        sec_copy.wait_recv()

    loads[2].wait()
    loads[3].wait()
    send_qg(0)
    for h in range(1, own_heads):
        send_kv(h)
        send_qg(h)

    def forward(h):
        for j in range(1, cols_n):
            kv_copy(h, j - 1).wait_recv()
            z_start(h, j)

    for j in range(cols_n - 1):
        bias_copy(j).wait_recv()

    nt = (((1,), (1,)), ((), ()))
    tn = (((0,), (0,)), ((), ()))

    def dot(a, b, dims):
        return lax.dot_general(a, b, dims, preferred_element_type=f32)

    def compute(h):
        @pl.loop(0, cols_n)
        def _(pair):
            query = qg_buf[h, pair, 0]
            grad = qg_buf[h, pair, 1]
            box = pl.ds(2 * pair, 4)
            key_rows = [kv_buf[h, i, 0, box].reshape(256, LANES) for i in range(3)]
            value_rows = [kv_buf[h, i, 1, box].reshape(256, LANES) for i in range(3)]
            blocks = []
            for i in range(3):
                part = dot(key_rows[i], query, nt) * scale
                for jj in range(4):
                    blocks.append(
                        part[jj * 64 : jj * 64 + 64] + bias_buf[pair, pl.ds(4 * i + jj, 1), :]
                    )
            scores = jnp.concatenate(blocks, axis=0)
            weights = jnp.exp2(scores - jnp.max(scores, axis=0, keepdims=True))
            probs = weights * (1.0 / jnp.sum(weights, axis=0, keepdims=True))
            low = probs.astype(bf16)
            grad_probs = jnp.concatenate([dot(rows, grad, nt) for rows in value_rows], axis=0)
            deltas = jnp.sum(low.astype(f32) * grad_probs, axis=0, keepdims=True)
            grad_scores = (probs * (grad_probs - deltas) * inv_root).astype(bf16)
            keys_all = jnp.concatenate(key_rows, axis=0)
            dq_send[h, pair] = dot(grad_scores, keys_all, tn).astype(bf16)
            grad_key = dot(grad_scores, query, (((1,), (0,)), ((), ())))
            grad_value = dot(low, grad, (((1,), (0,)), ((), ())))
            for i in range(3):
                at = slice(i * 256, i * 256 + 256)
                acc[h, i, 0, box] += grad_key[at].reshape(4, 64, LANES)
                acc[h, i, 1, box] += grad_value[at].reshape(4, 64, LANES)

            @pl.when(pair > 0)
            def _():
                dz_start(h, pair - 1)

        dz_start(h, cols_n - 1)

    def finish(h):
        @pl.loop(0, cols_n)
        def _(pair):
            @pl.when(has_down)
            def _():
                dz_copy(h, pair, 0).wait_recv()

            @pl.when(has_up)
            def _():
                dz_copy(h, pair, 1).wait_recv()

            for kv in range(2):
                total = (
                    acc[h, 1, kv, pl.ds(1 + 2 * pair, 2)]
                    + dz_recv[h, 0, kv, pl.ds(2 * pair, 2)].astype(f32)
                    + dz_recv[h, 1, kv, pl.ds(2 * pair, 2)].astype(f32)
                )
                dkv_send[h, pair, kv] = total.astype(bf16).reshape(128, LANES)

            @pl.when(pair != col)
            def _():
                dkv_copy(h, lax.rem(pair - col + cols_n - 1, cols_n)).start()

        dkv_recv[col * own_heads + h] = dkv_send[h, col]

    forward(0)
    for h in range(own_heads):
        if h + 1 < own_heads:
            forward(h + 1)
        for j in range(cols_n - 1):
            qg_copy(h, j).wait_recv()

        @pl.when(has_down)
        def _(h=h):
            for j in range(cols_n):
                z_copy(h, j, 0).wait_recv()

        @pl.when(has_up)
        def _(h=h):
            for j in range(cols_n):
                z_copy(h, j, 1).wait_recv()

        compute(h)
        for j in range(cols_n - 1):
            dq_copy(h, j).start()
        dq_recv[col * own_heads + h] = dq_send[h, col]
        if h > 0:
            finish(h - 1)
    finish(own_heads - 1)

    for h in range(own_heads):
        for j in range(cols_n - 1):
            dq_copy(h, j).wait_recv()

    @pl.loop(0, HEADS)
    def _(head):
        oq_ref[:, head_cols(head)] = from_tiles(dq_recv[head].astype(f32)).astype(bf16)

    stores[0].start()

    def place(h):
        for j in range(cols_n - 1):
            dkv_copy(h, j).wait_recv()

        @pl.loop(0, cols_n)
        def _(peer):
            head = peer * own_heads + h
            at = head_cols(head)
            ok_ref[:, at] = from_tiles(dkv_recv[head, 0].astype(f32)).astype(bf16)
            ov_ref[:, at] = from_tiles(dkv_recv[head, 1].astype(f32)).astype(bf16)

    for h in range(own_heads):
        place(h)
    stores[1].start()
    stores[2].start()

    @pl.when(sec > 0)
    def _():
        sec_copy.wait_send()

    for j in range(cols_n - 1):
        bias_copy(j).wait_send()
        for h in range(own_heads):
            for copy in (kv_copy, qg_copy, dq_copy, dkv_copy):
                copy(h, j).wait_send()
    for d, cond in ((0, has_up), (1, has_down)):
        @pl.when(cond)
        def _(d=d):
            for h in range(own_heads):
                for j in range(cols_n):
                    z_copy(h, j, d).wait_send()
                    dz_copy(h, j, d).wait_send()
    for store in stores:
        store.wait()


def fused_body(queries, keys, values, cotangent, upstream, block_mask):
    sections, rows_n, cols_n = (lax.axis_size(a) for a in ("section", "ha", "wa"))
    shape = queries.shape
    tokens = shape[1] * shape[2] * shape[3]
    flat = (tokens, shape[4])
    own = HEADS // cols_n
    tiles = 2 * cols_n
    bf16, f32 = jnp.bfloat16, jnp.float32
    dma = pltpu.SemaphoreType.DMA
    out = pl.pallas_call(
        functools.partial(fused_kernel, sections, rows_n, cols_n),
        out_shape=[jax.ShapeDtypeStruct(flat, bf16)] * 3,
        in_specs=[pl.BlockSpec(memory_space=pltpu.HBM)] * 6,
        out_specs=[pl.BlockSpec(memory_space=pltpu.HBM)] * 3,
        scratch_shapes=[
            pltpu.VMEM(flat, bf16),
            pltpu.VMEM((HEADS, 2, 2, 64, LANES), bf16),
            pltpu.VMEM((HEADS, 2, 128, LANES), bf16),
            pltpu.VMEM((16, LANES), f32),
            pltpu.VMEM((own, 3, 2, tiles + 2, 64, LANES), bf16),
            pltpu.VMEM((own, cols_n, 2, 128, LANES), bf16),
            pltpu.VMEM((cols_n, 16, LANES), f32),
            pltpu.VMEM((own, 3, 2, tiles + 2, 64, LANES), f32),
            pltpu.VMEM((own, 2, 2, tiles, 64, LANES), bf16),
            pltpu.VMEM((own, 2, 2, tiles, 64, LANES), bf16),
            pltpu.VMEM((own, cols_n, 128, LANES), bf16),
            pltpu.VMEM((HEADS, 128, LANES), bf16),
            pltpu.VMEM((own, cols_n, 2, 128, LANES), bf16),
            pltpu.VMEM((HEADS, 2, 128, LANES), bf16),
            pltpu.VMEM(flat, bf16),
            pltpu.VMEM(flat, bf16),
            pltpu.VMEM(flat, bf16),
            pltpu.VMEM(flat, bf16),
            pltpu.SMEM((2, 9), jnp.int32),
            dma((5,)),
            pltpu.VMEM(flat, bf16),
            pltpu.VMEM(flat, bf16),
            pltpu.VMEM(flat, bf16),
            dma((3,)),
            dma((2,)),
            dma((2, own, cols_n - 1)),
            dma((2, own, cols_n - 1)),
            dma((2, cols_n - 1)),
            dma((2, own, cols_n, 2)),
            dma((2, own, cols_n, 2)),
            dma((2, own, cols_n - 1)),
            dma((2, own, cols_n - 1)),
        ],
        compiler_params=pltpu.CompilerParams(
            collective_id=0, has_side_effects=True, vmem_limit_bytes=62 * 2**20
        ),
    )(
        queries.reshape(flat), keys.reshape(flat), values.reshape(flat),
        cotangent.reshape(flat), upstream.reshape(flat), block_mask.reshape(2, 9),
    )
    return tuple(x.reshape(shape) for x in out)


def solution(mesh):
    fits = mesh.shape["wa"] == 4
    return jax.shard_map(
        fused_body if fits else body,
        mesh=mesh,
        in_specs=(
            P("section", None, "ha", "wa", None),
            P("section", None, "ha", "wa", None),
            P("section", None, "ha", "wa", None),
            P("section", None, "ha", "wa", None),
            P("section", None, "ha", "wa", None),
            P("section", "ha", "wa", None),
        ),
        out_specs=(
            P("section", None, "ha", "wa", None),
            P("section", None, "ha", "wa", None),
            P("section", None, "ha", "wa", None),
        ),
        check_vma=False,
    )
```
